32 devices in a mesh: groups: 2 (over y), rows: 4 (over x, core), cols: 4 (over z).
Axes of the slice: x: 2, y: 2, z: 4, core: 2. Of those that a mesh axis runs over, the one named last changes fastest.
Arguments:
- query: bfloat16 [4096, 8192], P(('groups', 'rows'), 'cols'), parts along dimension 0, may hold values from -6 to 6
- keys: bfloat16 [4096, 8192], P(('groups', 'rows'), 'cols'), parts along dimension 0, may hold values from -6 to 6
- values: bfloat16 [4096, 8192], P(('groups', 'rows'), 'cols'), parts along dimension 0, may hold values from -6 to 6
- taps: float32 [128, 8192], P(None, 'cols'), may hold values from -1.25 to 1.25
- weight: bfloat16 [8192, 8192], P('rows', 'cols'), may hold values from -0.0625 to 0.0625
- doc_lengths: int32 [32], P('groups'), parts along dimension 0, may hold values from 1 to 512, 2048 in all
Outputs:
- projected: bfloat16 [4096, 8192], P(('groups', 'rows'), 'cols'), parts along dimension 0
The draws below stay inside these ranges and needn't reach their ends.
There are 2 independent parts, one for each index of `groups`. The reference program is written for one: setup_inputs(seed, part) draws one part's arguments, and reference() takes and returns one part's arrays. A program takes and returns all parts, laid end to end along the dimension named above; an argument that names none is the same for every part. Nothing has to cross between parts.
Inputs may be any that keep to these rules, and one draw needn't show every extreme that they name: `doc_lengths`: the lengths sum to 2048; the longest document has exactly 512 tokens.
All inputs are finite; a program needn't handle non-finite values.
Results may differ from the reference program's by a relative error of at most 0.0057.
Values may be sent and summed in bfloat16 or wider, within the bound.
A program may use at most 128 MiB of HBM per device.

```python
import math
import jax
import jax.numpy as jnp
import numpy as np
from jax import lax

D = 8192
TAPS = 128
NDOC = 16
LENGTH = 2048


def block_levels(key, extent, shards, smallest, high):
    def one(position, parts):
        heights = jax.random.uniform(jax.random.fold_in(jax.random.fold_in(key, 6), position), (parts,), jnp.float32, smallest / len(shards), high / len(shards))
        return jnp.repeat(jnp.exp(heights), extent[position] // parts).reshape((-1,) + (1,) * (len(extent) - position - 1))

    level = one(*shards[0])
    for cut in shards[1:]:
        level = level * one(*cut)
    return level


def profile(amount, total, bound, slope):
    weights = [(1 << 20) // math.isqrt(rank ** slope) + 1 for rank in range(2, amount + 1)]
    spare, counts = total - bound - (amount - 1), [1] * (amount - 1)
    while spare > 0:
        movable = [i for i in range(amount - 1) if counts[i] < bound]
        pool, left = sum([weights[i] for i in movable]), spare
        for i in movable:
            more = min(bound - counts[i], max(1, left * weights[i] // pool), spare)
            counts[i] = counts[i] + more
            spare = spare - more
    return np.array([bound] + counts)


def ragged(own_key, number_of, total, most, skew):
    if number_of == 2:
        one = jax.random.randint(own_key, (), max(1, total - most), min(most, total - 1) + 1)
        return jnp.stack([one, total - one])
    tallies = jnp.asarray(profile(number_of, total, most, skew), jnp.int32)
    pairs = (number_of - 1) // 2
    source_of, taker = tallies[1:1 + 2 * pairs:2], tallies[2:2 + 2 * pairs:2]
    room = jnp.minimum(source_of - 1, most - taker)
    shifted = jax.random.randint(jax.random.fold_in(own_key, 1), (pairs,), 0, 1 << 20) % (room + 1)
    tallies = tallies.at[1:1 + 2 * pairs:2].set(source_of - shifted).at[2:2 + 2 * pairs:2].set(taker + shifted)
    return tallies[jax.random.permutation(jax.random.fold_in(own_key, 2), number_of)]


def normal_values(rng, extent, width, reach, cuts=(), dtype=jnp.bfloat16):
    entries = width * jax.random.normal(rng, extent, jnp.float32)
    if cuts:
        entries = entries * block_levels(rng, extent, cuts, -0.22, 0.18)
    return jnp.clip(entries, -reach, reach).astype(dtype)


def setup_inputs(seed: int = 0, part: int = 0) -> dict:
    streams_of = jax.random.split(jax.random.key(seed), 7)
    part_keys = jax.random.split(jax.random.fold_in(streams_of[6], part), 7)
    query = normal_values(part_keys[0], (LENGTH, D), 1.0, 6.0, ((0, 4), (1, 4)))
    keys = normal_values(part_keys[1], (LENGTH, D), 1.0, 6.0, ((0, 4), (1, 4)))
    values = normal_values(part_keys[2], (LENGTH, D), 1.0, 6.0, ((0, 4), (1, 4)))
    taps = normal_values(streams_of[3], (TAPS, D), (TAPS ** -0.5), 1.25, ((1, 4),), jnp.float32)
    weight = normal_values(streams_of[4], (D, D), D ** -0.5, 0.0625, ((0, 4), (1, 4)))
    doc_lengths = ragged(part_keys[5], NDOC, LENGTH, LENGTH // 4, 2).astype(jnp.int32)
    return dict(query=query, keys=keys, values=values, taps=taps, weight=weight, doc_lengths=doc_lengths)


def reference(query, keys, values, taps, weight, doc_lengths):
    product = (keys.astype(jnp.float32) * values.astype(jnp.float32)).astype(jnp.bfloat16)
    ends = jnp.cumsum(doc_lengths).astype(jnp.int32)
    places = jnp.arange(LENGTH).astype(jnp.int32)
    segment = jnp.sum((ends[None, :] <= places[:, None]).astype(jnp.int32), axis=1).astype(jnp.int32)
    span = TAPS - 1
    extended = jnp.concatenate([jnp.zeros((span, D), jnp.bfloat16), product], axis=0)
    seg_ext = jnp.concatenate([jnp.full((span,), -1, jnp.int32), segment], axis=0)

    def one_tap(j, total):
        offset = (span - j).astype(jnp.int32)
        window = lax.dynamic_slice_in_dim(extended, offset, LENGTH, 0).astype(jnp.float32)
        seg_win = lax.dynamic_slice_in_dim(seg_ext, offset, LENGTH, 0)
        tap_row = lax.dynamic_index_in_dim(taps, j, 0, keepdims=False)
        return total + jnp.where((seg_win == segment)[:, None], tap_row[None, :] * window, jnp.float32(0.0))

    filtered = lax.fori_loop(0, TAPS, one_tap, jnp.zeros((LENGTH, D), jnp.float32))
    gated = (query.astype(jnp.float32) * filtered).astype(jnp.bfloat16)
    return jnp.dot(gated, weight, preferred_element_type=jnp.float32).astype(jnp.bfloat16)
```

```python
import functools

import jax
import jax.numpy as jnp
from jax import lax
from jax.experimental import pallas as pl
from jax.experimental.pallas import tpu as pltpu
from jax.sharding import PartitionSpec as P

MESH = pl.DeviceIdType.MESH
BT = 16
CT = 64
WCH = 8


def conv_block(b, start_ref, xs, hs, ys, n_taps):
    head = start_ref[b] - b

    def history(i, acc):
        k = n_taps // BT - i
        lo = jnp.full((8, 128), head + k * BT, jnp.int32)
        base = n_taps + b - k * BT
        taps = [
            hs[pl.ds(pl.multiple_of((k * BT + d) * 8, 8), 8), :] for d in range(1 - BT, BT)
        ]
        acc = list(acc)
        for s in range(BT):
            x = xs[pl.ds(pl.multiple_of((base + s) * 8, 8), 8), :]
            x = jnp.where(lo <= s, x, 0.0)
            for t in range(BT):
                acc[t] = acc[t] + taps[t - s + BT - 1] * x
        return tuple(acc)

    zero = jnp.zeros((8, 128), jnp.float32)
    acc = lax.fori_loop(0, n_taps // BT, history, (zero,) * BT)
    xb = [xs[pl.ds(pl.multiple_of((n_taps + b + s) * 8, 8), 8), :] for s in range(BT)]
    for t in range(BT):
        lo = jnp.full((8, 128), start_ref[b + t] - b, jnp.int32)
        total = jnp.where(lo < 0, acc[t], 0.0)
        for s in range(t + 1):
            term = hs[(t - s) * 8 : (t - s) * 8 + 8, :] * xb[s]
            total = total + (term if s == t else jnp.where(lo <= s, term, 0.0))
        ys[t * 8 : t * 8 + 8, :] = total


def kernel(dims, q_hbm, k_hbm, v_hbm, w_hbm, taps_hbm, start_ref, out, tok, wbuf, acc, xs, hs, ys,
           qs, ks, vs, ts, ktail, vtail, hsend, halo, in_sem, tail_sem, hsem, tsend, trecv, wsend, wrecv, ysend, yrecv, csend, crecv, osem):
    Z, X, T, C, CW, CG, TC, R, n_taps = dims
    NB = CG * TC
    z = lax.axis_index("cols")
    r = lax.axis_index("rows")
    y = lax.axis_index("groups")
    x, core = r // 2, r % 2
    mate = r + 1 - 2 * core
    half, RC = R // 2, R // 2 // WCH

    def load(cg):
        cols = pl.ds(cg * CW, CW)
        return [
            pltpu.make_async_copy(q_hbm.at[:, cols], qs.at[cg], in_sem.at[0, cg]),
            pltpu.make_async_copy(k_hbm.at[:, cols], ks, in_sem.at[1, cg]),
            pltpu.make_async_copy(v_hbm.at[:, cols], vs, in_sem.at[2, cg]),
            pltpu.make_async_copy(taps_hbm.at[:, cols], ts, in_sem.at[3, cg]),
        ]

    last_rows = pl.ds(T - n_taps, n_taps)
    tails = [
        pltpu.make_async_copy(k_hbm.at[last_rows], ktail, tail_sem.at[0]),
        pltpu.make_async_copy(v_hbm.at[last_rows], vtail, tail_sem.at[1]),
    ]
    for copy in tails:
        copy.start()

    for copy in load(0):
        copy.start()
    own_w = pltpu.make_async_copy(w_hbm, wbuf.at[pl.ds(r * R, R)], osem.at[0])
    own_w.start()
    acc[...] = jnp.zeros_like(acc)
    for copy in tails:
        copy.wait()
    tail = ktail[...].astype(jnp.float32) * vtail[...].astype(jnp.float32)
    hsend[...] = tail.astype(jnp.bfloat16)

    @pl.when(r == 0)
    def _():
        halo[...] = jnp.zeros_like(halo)

    barrier = pltpu.get_barrier_semaphore()

    def greet(cond, who):
        @pl.when(cond)
        def _():
            pl.semaphore_signal(barrier, inc=1, device_id=who, device_id_type=MESH)

    greet(z > 0, {"cols": z - 1})
    greet(z < Z - 1, {"cols": z + 1})
    greet(x > 0, {"rows": r - 2})
    greet(x < X - 1, {"rows": r + 2})
    greet((core == 0) & (x > 0), {"rows": r - 1})
    greet((core == 1) & (x < X - 1), {"rows": r + 1})
    pl.semaphore_signal(barrier, inc=1, device_id={"rows": mate}, device_id_type=MESH)
    pl.semaphore_signal(barrier, inc=1, device_id={"groups": 1 - y}, device_id_type=MESH)
    ends = jnp.where(z == 0, 1, 0) + jnp.where(z == Z - 1, 1, 0)
    ends = ends + jnp.where(x == 0, 1, 0) + jnp.where(x == X - 1, 1, 0)
    ends = ends + jnp.where((x == 0) & (core == 0), 1, 0)
    ends = ends + jnp.where((x == X - 1) & (core == 1), 1, 0)
    pl.semaphore_wait(barrier, 7 - ends)

    def remote(src, dst, send, recv, who):
        return pltpu.make_async_remote_copy(
            src_ref=src, dst_ref=dst, send_sem=send, recv_sem=recv, device_id=who, device_id_type=MESH
        )

    def h_copy():
        return remote(hsend, halo, hsem.at[0], hsem.at[1], {"rows": r + 1})

    @pl.when(r < 2 * X - 1)
    def _():
        h_copy().start()

    def wrows(rb, h, j):
        return pl.ds(pl.multiple_of(rb * R + h * half + j * RC, 16), RC)

    def x_copy(xb, j, step, own=False):
        rows = wrows(2 * xb + core, y, j)
        src = w_hbm.at[pl.ds(pl.multiple_of(y * half + j * RC, 16), RC)] if own else wbuf.at[rows]
        lane = 0 if step > 0 else 1
        return remote(src, wbuf.at[rows], wsend.at[lane, xb, j], wrecv.at[xb, j], {"rows": r + 2 * step})

    def y_copy(xb, h, j):
        rows = wrows(2 * xb + core, h, j)
        return remote(wbuf.at[rows], wbuf.at[rows], ysend.at[xb, j], yrecv.at[xb, j], {"groups": 1 - y})

    def c_copy(xb, owner, h, j):
        rows = wrows(2 * xb + owner, h, j)
        return remote(wbuf.at[rows], wbuf.at[rows], csend.at[xb, h, j], crecv.at[xb, h, j], {"rows": mate})

    own_rows, mate_rows = pl.ds(r * R, R), pl.ds(mate * R, R)

    def own_copy(rows):
        return remote(w_hbm, wbuf.at[rows], osem.at[1], osem.at[2], {"rows": mate})

    def each(n, fn):
        lax.fori_loop(0, n, lambda i, c: (fn(i), c)[1], 0)

    def send_own_w(j):
        @pl.when(x < X - 1)
        def _():
            x_copy(x, j, 1, True).start()

        @pl.when(x > 0)
        def _():
            x_copy(x, j, -1, True).start()

    each(WCH, send_own_w)
    own_copy(own_rows).start()

    def w_step(e, j):
        def pass_on(xb, step, more):
            x_copy(xb, j, step).wait_recv()

            @pl.when(more)
            def _():
                x_copy(xb, j, step).start()

            y_copy(xb, y, j).start()
            c_copy(xb, core, y, j).start()

        @pl.when(x - e >= 0)
        def _():
            pass_on(x - e, 1, x < X - 1)

        @pl.when(x + e <= X - 1)
        def _():
            pass_on(x + e, -1, x > 0)

    def y_step(e, j):
        def pass_on(xb):
            y_copy(xb, 1 - y, j).wait_recv()
            c_copy(xb, core, 1 - y, j).start()

        @pl.when(x - e >= 0)
        def _():
            pass_on(x - e)

        @pl.when(x + e <= X - 1)
        def _():
            pass_on(x + e)

    def t_copy(b, n, step):
        part = tok.at[b, n]
        lane = 0 if step > 0 else 1
        return remote(part, part, tsend.at[lane, b, n], trecv.at[b, n], {"cols": z + step})

    def t_step(d, n):
        @pl.when(z - d >= 0)
        def _():
            t_copy(z - d, n, 1).wait_recv()

            @pl.when(z < Z - 1)
            def _():
                t_copy(z - d, n, 1).start()

        @pl.when(z + d <= Z - 1)
        def _():
            t_copy(z + d, n, -1).wait_recv()

            @pl.when(z > 0)
            def _():
                t_copy(z + d, n, -1).start()

    w_queue = [(w_step, e, j) for e in range(1, X) for j in range(WCH)]
    y_queue = [(y_step, e, j) for e in range(1, X) for j in range(WCH)]

    def pump():
        if w_queue:
            fn, e, j = w_queue.pop(0)
            fn(e, j)
            if len(y_queue) > len(w_queue) + 1:
                fn, e, j = y_queue.pop(0)
                fn(e, j)

    G = CW // 128
    hs[n_taps * 8 :, :] = jnp.zeros((BT * 8, 128), jnp.float32)
    sent, passed = [], 0
    back = n_taps // CT
    for cg in range(CG):
        for copy in load(cg):
            copy.wait()
        for g in range(G):
            hs[pl.ds(g, n_taps, stride=8), :] = ts[:, g * 128 : g * 128 + 128]

        def fill(tc):
            for g in range(G):
                cols = slice(g * 128, g * 128 + 128)
                rows = pl.ds(pl.multiple_of(tc * CT, CT), CT)
                prod = ks[rows, cols].astype(jnp.float32) * vs[rows, cols].astype(jnp.float32)
                prod = prod.astype(jnp.bfloat16).astype(jnp.float32)
                xs[pl.ds((n_taps + tc * CT) * 8 + g, CT, stride=8), :] = prod

        def chunk(tc, cg=cg):
            def block(i, c):
                b = tc * CT + i * BT
                conv_block(b, start_ref, xs, hs, ys, n_taps)
                rows = pl.ds(pl.multiple_of(b, BT), BT)
                here = pl.ds(pl.multiple_of(i * BT, BT), BT)
                for g in range(G):
                    cols = slice(g * 128, g * 128 + 128)
                    filtered = ys[pl.ds(g, BT, stride=8), :]
                    gate = qs[cg, rows, cols].astype(jnp.float32)
                    tok[z, cg * TC + tc, here, cols] = (gate * filtered).astype(jnp.bfloat16)
                return c

            lax.fori_loop(0, CT // BT, block, 0)

        each(back, fill)
        order = list(range(back, TC)) + list(range(back))
        for place, tc in enumerate(order):
            n = cg * TC + tc
            if tc >= back:
                fill(tc)
            if place == TC - back:
                if cg == 0:
                    @pl.when(r > 0)
                    def _():
                        h_copy().wait_recv()

                for g in range(G):
                    c0 = cg * CW + g * 128
                    xs[pl.ds(g, n_taps, stride=8), :] = halo[:, c0 : c0 + 128].astype(jnp.float32)
            if place == TC - back and cg + 1 < CG:
                for copy in load(cg + 1):
                    copy.start()
            chunk(tc)

            @pl.when(z < Z - 1)
            def _():
                t_copy(z, n, 1).start()

            @pl.when(z > 0)
            def _():
                t_copy(z, n, -1).start()

            sent.append(n)
            if len(sent) >= 6 and len(sent) % 3 == 0:
                t_step(1, sent[passed])
                passed += 1
            if len(sent) >= 7 and len(sent) % 3 == 1:
                pump()

    NT = min(C, 512)

    def matmul(b):
        for cg in range(CG):
            rows = pl.ds(pl.multiple_of(b * C + cg * CW, CW), CW)

            def tile(i, c, cg=cg):
                cols = pl.ds(pl.multiple_of(i * NT, NT), NT)
                lhs = tok[b, cg * TC : (cg + 1) * TC].reshape(T, CW)
                part = jnp.dot(lhs, wbuf[rows, cols], preferred_element_type=jnp.float32)
                acc[:, cols] += part
                return c

            lax.fori_loop(0, C // NT, tile, 0)

    def piece(b, cg, h):
        rows = pl.ds(pl.multiple_of(b * C + cg * CW, CW), CW)
        here = slice(h * (T // 2), (h + 1) * (T // 2))

        def tile(i, c):
            cols = pl.ds(pl.multiple_of(i * NT, NT), NT)
            first = cg * TC + h * (TC // 2)
            lhs = tok[b, first : first + TC // 2].reshape(T // 2, CW)
            acc[here, cols] += jnp.dot(lhs, wbuf[rows, cols], preferred_element_type=jnp.float32)
            return c

        lax.fori_loop(0, C // NT, tile, 0)

    def multiply(d, here):
        for b in [z] if d == 0 else [z - d, z + d]:
            mine = b // 2 == x

            @pl.when((b >= 0) & (b <= Z - 1) & (mine if here else jnp.logical_not(mine)))
            def _():
                matmul(b)

    for n in sent[passed:]:
        t_step(1, n)
    own_w.wait()
    own_copy(mate_rows).wait_recv()
    multiply(0, True)
    if Z > 2:
        multiply(1, True)
        pump()
        for place, n in enumerate(sent):
            if place in (NB // 2, NB - 3):
                pump()
            t_step(2, n)
    while w_queue:
        pump()
    for fn, e, j in y_queue:
        fn(e, j)

    for d in range(3, Z - 1):
        each(NB, functools.partial(t_step, d))

    for d in range(2, Z - 1):
        multiply(d, True)


    def c_wait(e, j):
        for sign in (-1, 1):
            xb = x + sign * e

            @pl.when((xb >= 0) & (xb <= X - 1))
            def _():
                for h in range(2):
                    c_copy(xb, 1 - core, h, j).wait_recv()

    for e in range(1, X):
        each(WCH, functools.partial(c_wait, e))

    for d in range(Z - 1):
        multiply(d, False)
    if Z == 2:
        multiply(1, True)
        multiply(1, False)
    d = Z - 1
    if d > 1:
        for part in range(2 * CG):
            cg, h = part // 2, 1 - part % 2
            for n in range(cg * TC + h * (TC // 2), cg * TC + (h + 1) * (TC // 2)):
                if d > 2:
                    t_step(d, n)

            @pl.when(z - d >= 0)
            def _():
                piece(z - d, cg, h)

            @pl.when(z + d <= Z - 1)
            def _():
                piece(z + d, cg, h)

    out[...] = acc[...].astype(jnp.bfloat16)

    def sent_own_w(j):
        @pl.when(x < X - 1)
        def _():
            x_copy(x, j, 1, True).wait_send()

        @pl.when(x > 0)
        def _():
            x_copy(x, j, -1, True).wait_send()

    @pl.when(r < 2 * X - 1)
    def _():
        h_copy().wait_send()

    each(WCH, sent_own_w)
    own_copy(own_rows).wait_send()

    def w_sent(e, j):
        def left(xb, step, more):
            @pl.when(more)
            def _():
                x_copy(xb, j, step).wait_send()

            y_copy(xb, y, j).wait_send()
            c_copy(xb, core, y, j).wait_send()
            c_copy(xb, core, 1 - y, j).wait_send()

        @pl.when(x - e >= 0)
        def _():
            left(x - e, 1, x < X - 1)

        @pl.when(x + e <= X - 1)
        def _():
            left(x + e, -1, x > 0)

    for e in range(1, X):
        each(WCH, functools.partial(w_sent, e))

    def t_sent(d, n):
        @pl.when((z - d >= 0) & (z < Z - 1))
        def _():
            t_copy(z - d, n, 1).wait_send()

        @pl.when((z + d <= Z - 1) & (z > 0))
        def _():
            t_copy(z + d, n, -1).wait_send()

    for d in range(Z):
        each(NB, functools.partial(t_sent, d))


def local(Z, X, query, keys, values, taps, weight, doc_lengths):
    T, C = query.shape
    R = weight.shape[0]
    n_taps = taps.shape[0]
    first = lax.axis_index("rows") * T
    places = first + jnp.arange(T)
    start, end = jnp.zeros_like(places), 0
    for i in range(doc_lengths.shape[0]):
        end = end + doc_lengths[i]
        start = jnp.where(end <= places, end, start)
    start = (start - first).astype(jnp.int32)

    CW = min(C, 1024)
    CG, TC = C // CW, T // CT
    NB = CG * TC
    dims = (Z, X, T, C, CW, CG, TC, R, n_taps)
    any_spec = pl.BlockSpec(memory_space=pl.ANY)
    vmem = pl.BlockSpec(memory_space=pltpu.VMEM)
    dma = pltpu.SemaphoreType.DMA
    return pl.pallas_call(
        functools.partial(kernel, dims),
        out_shape=pltpu.VMEM((T, C), jnp.bfloat16),
        in_specs=[any_spec] * 5 + [pl.BlockSpec(memory_space=pltpu.SMEM)],
        out_specs=vmem,
        scratch_shapes=[
            pltpu.VMEM((Z, NB, CT, CW), jnp.bfloat16),
            pltpu.VMEM((2 * X * R, C), jnp.bfloat16),
            pltpu.VMEM((T, C), jnp.float32),
            pltpu.VMEM(((n_taps + T) * 8, 128), jnp.float32),
            pltpu.VMEM(((n_taps + BT) * 8, 128), jnp.float32),
            pltpu.VMEM((BT * 8, 128), jnp.float32),
            pltpu.VMEM((CG, T, CW), jnp.bfloat16),
            pltpu.VMEM((T, CW), jnp.bfloat16),
            pltpu.VMEM((T, CW), jnp.bfloat16),
            pltpu.VMEM((n_taps, CW), jnp.float32),
            pltpu.VMEM((n_taps, C), jnp.bfloat16),
            pltpu.VMEM((n_taps, C), jnp.bfloat16),
            pltpu.VMEM((n_taps, C), jnp.bfloat16),
            pltpu.VMEM((n_taps, C), jnp.bfloat16),
            dma((4, CG)),
            dma((2,)),
            dma((2,)),
            dma((2, Z, NB)),
            dma((Z, NB)),
            dma((2, X, WCH)),
            dma((X, WCH)),
            dma((X, WCH)),
            dma((X, WCH)),
            dma((X, 2, WCH)),
            dma((X, 2, WCH)),
            dma((3,)),
        ],
        compiler_params=pltpu.CompilerParams(
            collective_id=0, has_side_effects=True, vmem_limit_bytes=60 * 2**20
        ),
    )(query, keys, values, weight, taps, start)


def solution(mesh):
    placed = (
        P(("groups", "rows"), "cols"),
        P(("groups", "rows"), "cols"),
        P(("groups", "rows"), "cols"),
        P(None, "cols"),
        P("rows", "cols"),
        P("groups"),
    )
    run = functools.partial(local, mesh.shape["cols"], mesh.shape["rows"] // 2)
    return jax.shard_map(
        run, mesh=mesh, in_specs=placed, out_specs=P(("groups", "rows"), "cols"), check_vma=False
    )
```

```python
import functools

import jax
import jax.numpy as jnp
from jax import lax
from jax.experimental import pallas as pl
from jax.experimental.pallas import tpu as pltpu
from jax.sharding import PartitionSpec as P

MESH = pl.DeviceIdType.MESH
BT = 16
CT = 64
WCH = 8


def conv_block(b, start_ref, xs, hs, ys, n_taps):
    head = start_ref[b] - b

    def history(i, acc):
        k = n_taps // BT - i
        lo = jnp.full((8, 128), head + k * BT, jnp.int32)
        base = n_taps + b - k * BT
        taps = [
            hs[pl.ds(pl.multiple_of((k * BT + d) * 8, 8), 8), :] for d in range(1 - BT, BT)
        ]
        acc = list(acc)
        for s in range(BT):
            x = xs[pl.ds(pl.multiple_of((base + s) * 8, 8), 8), :]
            x = jnp.where(lo <= s, x, 0.0)
            for t in range(BT):
                acc[t] = acc[t] + taps[t - s + BT - 1] * x
        return tuple(acc)

    zero = jnp.zeros((8, 128), jnp.float32)
    acc = lax.fori_loop(0, n_taps // BT, history, (zero,) * BT)
    xb = [xs[pl.ds(pl.multiple_of((n_taps + b + s) * 8, 8), 8), :] for s in range(BT)]
    for t in range(BT):
        lo = jnp.full((8, 128), start_ref[b + t] - b, jnp.int32)
        total = jnp.where(lo < 0, acc[t], 0.0)
        for s in range(t + 1):
            term = hs[(t - s) * 8 : (t - s) * 8 + 8, :] * xb[s]
            total = total + (term if s == t else jnp.where(lo <= s, term, 0.0))
        ys[t * 8 : t * 8 + 8, :] = total


def kernel(dims, q_hbm, k_hbm, v_hbm, w_hbm, taps_hbm, start_ref, out, tok, wbuf, acc, xs, hs, ys,
           qs, ks, vs, ts, ktail, vtail, hsend, halo, in_sem, tail_sem, hsem, tsend, trecv, wsend, wrecv, ysend, yrecv, csend, crecv, osem):
    Z, X, T, C, CW, CG, TC, R, n_taps = dims
    NB = CG * TC
    z = lax.axis_index("cols")
    r = lax.axis_index("rows")
    y = lax.axis_index("groups")
    x, core = r // 2, r % 2
    mate = r + 1 - 2 * core
    half, RC = R // 2, R // 2 // WCH

    def load(cg):
        cols = pl.ds(cg * CW, CW)
        return [
            pltpu.make_async_copy(q_hbm.at[:, cols], qs.at[cg], in_sem.at[0, cg]),
            pltpu.make_async_copy(k_hbm.at[:, cols], ks, in_sem.at[1, cg]),
            pltpu.make_async_copy(v_hbm.at[:, cols], vs, in_sem.at[2, cg]),
            pltpu.make_async_copy(taps_hbm.at[:, cols], ts, in_sem.at[3, cg]),
        ]

    last_rows = pl.ds(T - n_taps, n_taps)
    tails = [
        pltpu.make_async_copy(k_hbm.at[last_rows], ktail, tail_sem.at[0]),
        pltpu.make_async_copy(v_hbm.at[last_rows], vtail, tail_sem.at[1]),
    ]
    for copy in tails:
        copy.start()

    for copy in load(0):
        copy.start()
    own_w = pltpu.make_async_copy(w_hbm, wbuf.at[pl.ds(r * R, R)], osem.at[0])
    own_w.start()
    acc[...] = jnp.zeros_like(acc)
    for copy in tails:
        copy.wait()
    tail = ktail[...].astype(jnp.float32) * vtail[...].astype(jnp.float32)
    hsend[...] = tail.astype(jnp.bfloat16)

    @pl.when(r == 0)
    def _():
        halo[...] = jnp.zeros_like(halo)

    barrier = pltpu.get_barrier_semaphore()

    def greet(cond, who):
        @pl.when(cond)
        def _():
            pl.semaphore_signal(barrier, inc=1, device_id=who, device_id_type=MESH)

    greet(z > 0, {"cols": z - 1})
    greet(z < Z - 1, {"cols": z + 1})
    greet(x > 0, {"rows": r - 2})
    greet(x < X - 1, {"rows": r + 2})
    greet((core == 0) & (x > 0), {"rows": r - 1})
    greet((core == 1) & (x < X - 1), {"rows": r + 1})
    pl.semaphore_signal(barrier, inc=1, device_id={"rows": mate}, device_id_type=MESH)
    pl.semaphore_signal(barrier, inc=1, device_id={"groups": 1 - y}, device_id_type=MESH)
    ends = jnp.where(z == 0, 1, 0) + jnp.where(z == Z - 1, 1, 0)
    ends = ends + jnp.where(x == 0, 1, 0) + jnp.where(x == X - 1, 1, 0)
    ends = ends + jnp.where((x == 0) & (core == 0), 1, 0)
    ends = ends + jnp.where((x == X - 1) & (core == 1), 1, 0)
    pl.semaphore_wait(barrier, 7 - ends)

    def remote(src, dst, send, recv, who):
        return pltpu.make_async_remote_copy(
            src_ref=src, dst_ref=dst, send_sem=send, recv_sem=recv, device_id=who, device_id_type=MESH
        )

    def h_copy():
        return remote(hsend, halo, hsem.at[0], hsem.at[1], {"rows": r + 1})

    @pl.when(r < 2 * X - 1)
    def _():
        h_copy().start()

    def wrows(rb, h, j):
        return pl.ds(pl.multiple_of(rb * R + h * half + j * RC, 16), RC)

    def x_copy(xb, j, step, own=False):
        rows = wrows(2 * xb + core, y, j)
        src = w_hbm.at[pl.ds(pl.multiple_of(y * half + j * RC, 16), RC)] if own else wbuf.at[rows]
        lane = 0 if step > 0 else 1
        return remote(src, wbuf.at[rows], wsend.at[lane, xb, j], wrecv.at[xb, j], {"rows": r + 2 * step})

    def y_copy(xb, h, j):
        rows = wrows(2 * xb + core, h, j)
        return remote(wbuf.at[rows], wbuf.at[rows], ysend.at[xb, j], yrecv.at[xb, j], {"groups": 1 - y})

    def c_copy(xb, owner, h, j):
        rows = wrows(2 * xb + owner, h, j)
        return remote(wbuf.at[rows], wbuf.at[rows], csend.at[xb, h, j], crecv.at[xb, h, j], {"rows": mate})

    own_rows, mate_rows = pl.ds(r * R, R), pl.ds(mate * R, R)

    def own_copy(rows):
        return remote(w_hbm, wbuf.at[rows], osem.at[1], osem.at[2], {"rows": mate})

    def each(n, fn):
        lax.fori_loop(0, n, lambda i, c: (fn(i), c)[1], 0)

    def send_own_w(j):
        @pl.when(x < X - 1)
        def _():
            x_copy(x, j, 1, True).start()

        @pl.when(x > 0)
        def _():
            x_copy(x, j, -1, True).start()

    each(WCH, send_own_w)
    own_copy(own_rows).start()

    def w_step(e, j):
        def pass_on(xb, step, more):
            x_copy(xb, j, step).wait_recv()

            @pl.when(more)
            def _():
                x_copy(xb, j, step).start()

            y_copy(xb, y, j).start()
            c_copy(xb, core, y, j).start()

        @pl.when(x - e >= 0)
        def _():
            pass_on(x - e, 1, x < X - 1)

        @pl.when(x + e <= X - 1)
        def _():
            pass_on(x + e, -1, x > 0)

    def y_step(e, j):
        def pass_on(xb):
            y_copy(xb, 1 - y, j).wait_recv()
            c_copy(xb, core, 1 - y, j).start()

        @pl.when(x - e >= 0)
        def _():
            pass_on(x - e)

        @pl.when(x + e <= X - 1)
        def _():
            pass_on(x + e)

    def t_copy(b, n, step):
        part = tok.at[b, n]
        lane = 0 if step > 0 else 1
        return remote(part, part, tsend.at[lane, b, n], trecv.at[b, n], {"cols": z + step})

    def t_step(d, n):
        @pl.when(z - d >= 0)
        def _():
            t_copy(z - d, n, 1).wait_recv()

            @pl.when(z < Z - 1)
            def _():
                t_copy(z - d, n, 1).start()

        @pl.when(z + d <= Z - 1)
        def _():
            t_copy(z + d, n, -1).wait_recv()

            @pl.when(z > 0)
            def _():
                t_copy(z + d, n, -1).start()

    w_queue = [(w_step, e, j) for e in range(1, X) for j in range(WCH)]
    y_queue = [(y_step, e, j) for e in range(1, X) for j in range(WCH)]

    def pump():
        if w_queue:
            fn, e, j = w_queue.pop(0)
            fn(e, j)
            if len(y_queue) > len(w_queue) + 1:
                fn, e, j = y_queue.pop(0)
                fn(e, j)

    G = CW // 128
    hs[n_taps * 8 :, :] = jnp.zeros((BT * 8, 128), jnp.float32)
    sent, passed = [], 0
    back = n_taps // CT
    for cg in range(CG):
        for copy in load(cg):
            copy.wait()
        for g in range(G):
            hs[pl.ds(g, n_taps, stride=8), :] = ts[:, g * 128 : g * 128 + 128]

        def fill(tc):
            for g in range(G):
                cols = slice(g * 128, g * 128 + 128)
                rows = pl.ds(pl.multiple_of(tc * CT, CT), CT)
                prod = ks[rows, cols].astype(jnp.float32) * vs[rows, cols].astype(jnp.float32)
                prod = prod.astype(jnp.bfloat16).astype(jnp.float32)
                xs[pl.ds((n_taps + tc * CT) * 8 + g, CT, stride=8), :] = prod

        def chunk(tc, cg=cg):
            def block(i, c):
                b = tc * CT + i * BT
                conv_block(b, start_ref, xs, hs, ys, n_taps)
                rows = pl.ds(pl.multiple_of(b, BT), BT)
                here = pl.ds(pl.multiple_of(i * BT, BT), BT)
                for g in range(G):
                    cols = slice(g * 128, g * 128 + 128)
                    filtered = ys[pl.ds(g, BT, stride=8), :]
                    gate = qs[cg, rows, cols].astype(jnp.float32)
                    tok[z, cg * TC + tc, here, cols] = (gate * filtered).astype(jnp.bfloat16)
                return c

            lax.fori_loop(0, CT // BT, block, 0)

        each(back, fill)
        order = list(range(back, TC)) + list(range(back))
        for place, tc in enumerate(order):
            n = cg * TC + tc
            if tc >= back:
                fill(tc)
            if place == TC - back:
                if cg == 0:
                    @pl.when(r > 0)
                    def _():
                        h_copy().wait_recv()

                for g in range(G):
                    c0 = cg * CW + g * 128
                    xs[pl.ds(g, n_taps, stride=8), :] = halo[:, c0 : c0 + 128].astype(jnp.float32)
            if place == TC - back and cg + 1 < CG:
                for copy in load(cg + 1):
                    copy.start()
            chunk(tc)

            @pl.when(z < Z - 1)
            def _():
                t_copy(z, n, 1).start()

            @pl.when(z > 0)
            def _():
                t_copy(z, n, -1).start()

            sent.append(n)
            if len(sent) >= 6 and len(sent) % 3 == 0:
                t_step(1, sent[passed])
                passed += 1
            if len(sent) >= 7 and len(sent) % 3 == 1:
                pump()

    NT = min(C, 512)

    def matmul(b):
        for cg in range(CG):
            rows = pl.ds(pl.multiple_of(b * C + cg * CW, CW), CW)

            def tile(i, c, cg=cg):
                cols = pl.ds(pl.multiple_of(i * NT, NT), NT)
                lhs = tok[b, cg * TC : (cg + 1) * TC].reshape(T, CW)
                part = jnp.dot(lhs, wbuf[rows, cols], preferred_element_type=jnp.float32)
                acc[:, cols] += part
                return c

            lax.fori_loop(0, C // NT, tile, 0)

    def piece(b, cg, h):
        rows = pl.ds(pl.multiple_of(b * C + cg * CW, CW), CW)
        here = slice(h * (T // 2), (h + 1) * (T // 2))

        def tile(i, c):
            cols = pl.ds(pl.multiple_of(i * NT, NT), NT)
            first = cg * TC + h * (TC // 2)
            lhs = tok[b, first : first + TC // 2].reshape(T // 2, CW)
            acc[here, cols] += jnp.dot(lhs, wbuf[rows, cols], preferred_element_type=jnp.float32)
            return c

        lax.fori_loop(0, C // NT, tile, 0)

    def multiply(d, here):
        for b in [z] if d == 0 else [z - d, z + d]:
            mine = b // 2 == x

            @pl.when((b >= 0) & (b <= Z - 1) & (mine if here else jnp.logical_not(mine)))
            def _():
                matmul(b)

    for n in sent[passed:]:
        t_step(1, n)
    own_w.wait()
    own_copy(mate_rows).wait_recv()
    multiply(0, True)
    if Z > 2:
        multiply(1, True)
        pump()
        for place, n in enumerate(sent):
            if place in (NB // 2, NB - 3):
                pump()
            t_step(2, n)
    while w_queue:
        pump()
    for fn, e, j in y_queue:
        fn(e, j)

    for d in range(3, Z - 1):
        each(NB, functools.partial(t_step, d))

    for d in range(2, Z - 1):
        multiply(d, True)


    def c_wait(e, j):
        for sign in (-1, 1):
            xb = x + sign * e

            @pl.when((xb >= 0) & (xb <= X - 1))
            def _():
                for h in range(2):
                    c_copy(xb, 1 - core, h, j).wait_recv()

    for e in range(1, X):
        each(WCH, functools.partial(c_wait, e))

    for d in range(Z - 1):
        multiply(d, False)
    if Z == 2:
        multiply(1, True)
        multiply(1, False)
    d = Z - 1
    if d > 1:
        for part in range(2 * CG):
            cg, h = part // 2, 1 - part % 2
            for n in range(cg * TC + h * (TC // 2), cg * TC + (h + 1) * (TC // 2)):
                if d > 2:
                    t_step(d, n)

            @pl.when(z - d >= 0)
            def _():
                piece(z - d, cg, h)

            @pl.when(z + d <= Z - 1)
            def _():
                piece(z + d, cg, h)

    out[...] = acc[...].astype(jnp.bfloat16)

    def sent_own_w(j):
        @pl.when(x < X - 1)
        def _():
            x_copy(x, j, 1, True).wait_send()

        @pl.when(x > 0)
        def _():
            x_copy(x, j, -1, True).wait_send()

    @pl.when(r < 2 * X - 1)
    def _():
        h_copy().wait_send()

    each(WCH, sent_own_w)
    own_copy(own_rows).wait_send()

    def w_sent(e, j):
        def left(xb, step, more):
            @pl.when(more)
            def _():
                x_copy(xb, j, step).wait_send()

            y_copy(xb, y, j).wait_send()
            c_copy(xb, core, y, j).wait_send()
            c_copy(xb, core, 1 - y, j).wait_send()

        @pl.when(x - e >= 0)
        def _():
            left(x - e, 1, x < X - 1)

        @pl.when(x + e <= X - 1)
        def _():
            left(x + e, -1, x > 0)

    for e in range(1, X):
        each(WCH, functools.partial(w_sent, e))

    def t_sent(d, n):
        @pl.when((z - d >= 0) & (z < Z - 1))
        def _():
            t_copy(z - d, n, 1).wait_send()

        @pl.when((z + d <= Z - 1) & (z > 0))
        def _():
            t_copy(z + d, n, -1).wait_send()

    for d in range(Z):
        each(NB, functools.partial(t_sent, d))


def local(Z, X, query, keys, values, taps, weight, doc_lengths):
    T, C = query.shape
    R = weight.shape[0]
    n_taps = taps.shape[0]
    first = lax.axis_index("rows") * T
    ids = jnp.arange(doc_lengths.shape[0])
    ends = jnp.sum(jnp.where(ids[None, :] <= ids[:, None], doc_lengths[None, :], 0), axis=1)
    places = first + jnp.arange(T)
    start = jnp.max(jnp.where(ends[None, :] <= places[:, None], ends[None, :], 0), axis=1)
    start = (start - first).astype(jnp.int32)

    CW = min(C, 1024)
    CG, TC = C // CW, T // CT
    NB = CG * TC
    dims = (Z, X, T, C, CW, CG, TC, R, n_taps)
    any_spec = pl.BlockSpec(memory_space=pl.ANY)
    vmem = pl.BlockSpec(memory_space=pltpu.VMEM)
    dma = pltpu.SemaphoreType.DMA
    return pl.pallas_call(
        functools.partial(kernel, dims),
        out_shape=pltpu.VMEM((T, C), jnp.bfloat16),
        in_specs=[any_spec] * 5 + [pl.BlockSpec(memory_space=pltpu.SMEM)],
        out_specs=vmem,
        scratch_shapes=[
            pltpu.VMEM((Z, NB, CT, CW), jnp.bfloat16),
            pltpu.VMEM((2 * X * R, C), jnp.bfloat16),
            pltpu.VMEM((T, C), jnp.float32),
            pltpu.VMEM(((n_taps + T) * 8, 128), jnp.float32),
            pltpu.VMEM(((n_taps + BT) * 8, 128), jnp.float32),
            pltpu.VMEM((BT * 8, 128), jnp.float32),
            pltpu.VMEM((CG, T, CW), jnp.bfloat16),
            pltpu.VMEM((T, CW), jnp.bfloat16),
            pltpu.VMEM((T, CW), jnp.bfloat16),
            pltpu.VMEM((n_taps, CW), jnp.float32),
            pltpu.VMEM((n_taps, C), jnp.bfloat16),
            pltpu.VMEM((n_taps, C), jnp.bfloat16),
            pltpu.VMEM((n_taps, C), jnp.bfloat16),
            pltpu.VMEM((n_taps, C), jnp.bfloat16),
            dma((4, CG)),
            dma((2,)),
            dma((2,)),
            dma((2, Z, NB)),
            dma((Z, NB)),
            dma((2, X, WCH)),
            dma((X, WCH)),
            dma((X, WCH)),
            dma((X, WCH)),
            dma((X, 2, WCH)),
            dma((X, 2, WCH)),
            dma((3,)),
        ],
        compiler_params=pltpu.CompilerParams(
            collective_id=0, has_side_effects=True, vmem_limit_bytes=60 * 2**20
        ),
    )(query, keys, values, weight, taps, start)


def solution(mesh):
    placed = (
        P(("groups", "rows"), "cols"),
        P(("groups", "rows"), "cols"),
        P(("groups", "rows"), "cols"),
        P(None, "cols"),
        P("rows", "cols"),
        P("groups"),
    )
    run = functools.partial(local, mesh.shape["cols"], mesh.shape["rows"] // 2)
    return jax.shard_map(
        run, mesh=mesh, in_specs=placed, out_specs=P(("groups", "rows"), "cols"), check_vma=False
    )
```

```python
import functools

import jax
import jax.numpy as jnp
from jax import lax
from jax.experimental import pallas as pl
from jax.experimental.pallas import tpu as pltpu
from jax.sharding import PartitionSpec as P

MESH = pl.DeviceIdType.MESH
BT = 16
CT = 64
WCH = 8


def conv_block(b, starts, xs, hs, ys, n_taps):
    head = jnp.broadcast_to(starts[pl.ds(b, 1), :], (8, 128)) - b

    def history(i, acc):
        k = n_taps // BT - i
        lo = head + k * BT
        base = n_taps + b - k * BT
        taps = [
            hs[pl.ds(pl.multiple_of((k * BT + d) * 8, 8), 8), :] for d in range(1 - BT, BT)
        ]
        acc = list(acc)
        for s in range(BT):
            x = xs[pl.ds(pl.multiple_of((base + s) * 8, 8), 8), :]
            x = jnp.where(lo <= s, x, 0.0)
            for t in range(BT):
                acc[t] = acc[t] + taps[t - s + BT - 1] * x
        return tuple(acc)

    zero = jnp.zeros((8, 128), jnp.float32)
    acc = lax.fori_loop(0, n_taps // BT, history, (zero,) * BT)
    xb = [xs[pl.ds(pl.multiple_of((n_taps + b + s) * 8, 8), 8), :] for s in range(BT)]
    for t in range(BT):
        lo = jnp.broadcast_to(starts[pl.ds(b + t, 1), :], (8, 128)) - b
        total = jnp.where(lo < 0, acc[t], 0.0)
        for s in range(t + 1):
            term = hs[(t - s) * 8 : (t - s) * 8 + 8, :] * xb[s]
            total = total + (term if s == t else jnp.where(lo <= s, term, 0.0))
        ys[t * 8 : t * 8 + 8, :] = total


def kernel(dims, q_hbm, k_hbm, v_hbm, w_hbm, taps_hbm, doc_ref, out, starts, tok, wbuf, acc, xs, hs, ys,
           qs, ks, vs, ts, ktail, vtail, hsend, halo, in_sem, tail_sem, hsem, tsend, trecv, wsend, wrecv, ysend, yrecv, csend, crecv, osem):
    Z, X, T, C, CW, CG, TC, R, n_taps = dims
    NB = CG * TC
    z = lax.axis_index("cols")
    r = lax.axis_index("rows")
    y = lax.axis_index("groups")
    x, core = r // 2, r % 2
    mate = r + 1 - 2 * core
    half, RC = R // 2, R // 2 // WCH

    EARLY = n_taps + CT

    def load(cg):
        cols = pl.ds(cg * CW, CW)
        copies = []
        for part, rows in enumerate((pl.ds(0, EARLY), pl.ds(EARLY, T - EARLY))):
            for i, (src, dst) in enumerate(((k_hbm, ks), (v_hbm, vs), (q_hbm, qs.at[cg]))):
                copies.append((src.at[rows, cols], dst.at[rows], in_sem.at[part, i, cg]))
            if part == 0:
                copies.append((taps_hbm.at[:, cols], ts, in_sem.at[0, 3, cg]))
        return copies

    def begin(copies):
        for src, dst, sem in copies:
            pltpu.make_async_copy(src, dst, sem).start()

    def finish(copies):
        for src, dst, sem in copies:
            pltpu.make_async_copy(src, dst, sem).wait()

    last_rows = pl.ds(T - n_taps, n_taps)
    tails = [
        pltpu.make_async_copy(k_hbm.at[last_rows], ktail, tail_sem.at[0]),
        pltpu.make_async_copy(v_hbm.at[last_rows], vtail, tail_sem.at[1]),
    ]

    begin(load(0)[:4])

    barrier = pltpu.get_barrier_semaphore()

    def greet(cond, who):
        @pl.when(cond)
        def _():
            pl.semaphore_signal(barrier, inc=1, device_id=who, device_id_type=MESH)

    greet(z > 0, {"cols": z - 1})
    greet(z < Z - 1, {"cols": z + 1})
    greet(x > 0, {"rows": r - 2})
    greet(x < X - 1, {"rows": r + 2})
    greet((core == 0) & (x > 0), {"rows": r - 1})
    greet((core == 1) & (x < X - 1), {"rows": r + 1})
    pl.semaphore_signal(barrier, inc=1, device_id={"rows": mate}, device_id_type=MESH)
    pl.semaphore_signal(barrier, inc=1, device_id={"groups": 1 - y}, device_id_type=MESH)
    begin(load(0)[4:])
    for copy in tails:
        copy.start()

    ends = []
    for i in range(doc_ref.shape[0]):
        ends.append(doc_ref[i] + (ends[-1] if ends else 0))

    def mark(i, c):
        rows = pl.ds(pl.multiple_of(i * CT, CT), CT)
        place = lax.broadcasted_iota(jnp.int32, (CT, 128), 0) + (r * T + i * CT)
        start = jnp.zeros((CT, 128), jnp.int32)
        for end in ends:
            start = jnp.where(place >= end, end, start)
        starts[rows, :] = start - r * T
        return c

    lax.fori_loop(0, T // CT, mark, 0)

    spots = jnp.where(z == 0, 1, 0) + jnp.where(z == Z - 1, 1, 0)
    spots = spots + jnp.where(x == 0, 1, 0) + jnp.where(x == X - 1, 1, 0)
    spots = spots + jnp.where((x == 0) & (core == 0), 1, 0)
    spots = spots + jnp.where((x == X - 1) & (core == 1), 1, 0)
    pl.semaphore_wait(barrier, 7 - spots)

    def remote(src, dst, send, recv, who):
        return pltpu.make_async_remote_copy(
            src_ref=src, dst_ref=dst, send_sem=send, recv_sem=recv, device_id=who, device_id_type=MESH
        )

    def h_copy():
        return remote(hsend, halo, hsem.at[0], hsem.at[1], {"rows": r + 1})

    def wrows(rb, h, j):
        return pl.ds(pl.multiple_of(rb * R + h * half + j * RC, 16), RC)

    def x_copy(xb, j, step, own=False):
        rows = wrows(2 * xb + core, y, j)
        src = w_hbm.at[pl.ds(pl.multiple_of(y * half + j * RC, 16), RC)] if own else wbuf.at[rows]
        lane = 0 if step > 0 else 1
        return remote(src, wbuf.at[rows], wsend.at[lane, xb, j], wrecv.at[xb, j], {"rows": r + 2 * step})

    def y_copy(xb, h, j):
        rows = wrows(2 * xb + core, h, j)
        return remote(wbuf.at[rows], wbuf.at[rows], ysend.at[xb, j], yrecv.at[xb, j], {"groups": 1 - y})

    def c_copy(xb, owner, h, j):
        rows = wrows(2 * xb + owner, h, j)
        return remote(wbuf.at[rows], wbuf.at[rows], csend.at[xb, h, j], crecv.at[xb, h, j], {"rows": mate})

    own_rows, mate_rows = pl.ds(r * R, R), pl.ds(mate * R, R)

    def own_copy(rows):
        return remote(w_hbm, wbuf.at[rows], osem.at[1], osem.at[2], {"rows": mate})

    def each(n, fn):
        lax.fori_loop(0, n, lambda i, c: (fn(i), c)[1], 0)

    def send_own_w(j):
        @pl.when(x < X - 1)
        def _():
            x_copy(x, j, 1, True).start()

        @pl.when(x > 0)
        def _():
            x_copy(x, j, -1, True).start()

    own_w = pltpu.make_async_copy(w_hbm, wbuf.at[pl.ds(r * R, R)], osem.at[0])

    def send_others():
        for copy in tails:
            copy.wait()
        tail = ktail[...].astype(jnp.float32) * vtail[...].astype(jnp.float32)
        hsend[...] = tail.astype(jnp.bfloat16)

        @pl.when(r < 2 * X - 1)
        def _():
            h_copy().start()

        each(WCH, send_own_w)
        own_copy(own_rows).start()
        own_w.start()
        acc[...] = jnp.zeros_like(acc)

        @pl.when(r == 0)
        def _():
            halo[...] = jnp.zeros_like(halo)

    def w_step(e, j):
        def pass_on(xb, step, more):
            x_copy(xb, j, step).wait_recv()

            @pl.when(more)
            def _():
                x_copy(xb, j, step).start()

            y_copy(xb, y, j).start()
            c_copy(xb, core, y, j).start()

        @pl.when(x - e >= 0)
        def _():
            pass_on(x - e, 1, x < X - 1)

        @pl.when(x + e <= X - 1)
        def _():
            pass_on(x + e, -1, x > 0)

    def y_step(e, j):
        def pass_on(xb):
            y_copy(xb, 1 - y, j).wait_recv()
            c_copy(xb, core, 1 - y, j).start()

        @pl.when(x - e >= 0)
        def _():
            pass_on(x - e)

        @pl.when(x + e <= X - 1)
        def _():
            pass_on(x + e)

    def t_copy(b, n, step, rows=None):
        part = tok.at[b, n] if rows is None else tok.at[b, n, rows]
        lane = 0 if step > 0 else 1
        return remote(part, part, tsend.at[lane, b, n], trecv.at[b, n], {"cols": z + step})

    def send_own(n, rows):
        @pl.when(z < Z - 1)
        def _():
            t_copy(z, n, 1, rows).start()

        @pl.when(z > 0)
        def _():
            t_copy(z, n, -1, rows).start()

    def t_step(d, n):
        @pl.when(z - d >= 0)
        def _():
            t_copy(z - d, n, 1).wait_recv()

            @pl.when(z < Z - 1)
            def _():
                t_copy(z - d, n, 1).start()

        @pl.when(z + d <= Z - 1)
        def _():
            t_copy(z + d, n, -1).wait_recv()

            @pl.when(z > 0)
            def _():
                t_copy(z + d, n, -1).start()

    w_queue = [(w_step, e, j) for e in range(1, X) for j in range(WCH)]
    y_queue = [(y_step, e, j) for e in range(1, X) for j in range(WCH)]

    def pump():
        if w_queue:
            fn, e, j = w_queue.pop(0)
            fn(e, j)
            if len(y_queue) > len(w_queue) + 1:
                fn, e, j = y_queue.pop(0)
                fn(e, j)

    G = CW // 128
    hs[n_taps * 8 :, :] = jnp.zeros((BT * 8, 128), jnp.float32)
    sent, passed = [], 0
    back = n_taps // CT
    for cg in range(CG):
        finish(load(cg)[: 4 if cg == 0 else None])
        for g in range(G):
            hs[pl.ds(g, n_taps, stride=8), :] = ts[:, g * 128 : g * 128 + 128]

        def fill(tc):
            for g in range(G):
                cols = slice(g * 128, g * 128 + 128)
                rows = pl.ds(pl.multiple_of(tc * CT, CT), CT)
                prod = ks[rows, cols].astype(jnp.float32) * vs[rows, cols].astype(jnp.float32)
                prod = prod.astype(jnp.bfloat16).astype(jnp.float32)
                xs[pl.ds((n_taps + tc * CT) * 8 + g, CT, stride=8), :] = prod

        def chunk(tc, early, cg=cg):
            def block(i, c):
                b = tc * CT + i * BT
                conv_block(b, starts, xs, hs, ys, n_taps)
                rows = pl.ds(pl.multiple_of(b, BT), BT)
                here = pl.ds(pl.multiple_of(i * BT, BT), BT)
                for g in range(G):
                    cols = slice(g * 128, g * 128 + 128)
                    filtered = ys[pl.ds(g, BT, stride=8), :]
                    gate = qs[cg, rows, cols].astype(jnp.float32)
                    tok[z, cg * TC + tc, here, cols] = (gate * filtered).astype(jnp.bfloat16)
                if early:
                    send_own(cg * TC + tc, here)
                return c

            lax.fori_loop(0, CT // BT, block, 0)

        each(back, fill)
        order = list(range(back, TC)) + list(range(back))
        for place, tc in enumerate(order):
            n = cg * TC + tc
            if tc >= back:
                fill(tc)
            if place == TC - back:
                if cg == 0:
                    @pl.when(r > 0)
                    def _():
                        h_copy().wait_recv()

                for g in range(G):
                    c0 = cg * CW + g * 128
                    xs[pl.ds(g, n_taps, stride=8), :] = halo[:, c0 : c0 + 128].astype(jnp.float32)
            if place == TC - back and cg + 1 < CG:
                begin(load(cg + 1))
            early = cg == 0 and place == 0
            chunk(tc, early)
            if early:
                send_others()
                finish(load(0)[4:])
            else:
                send_own(n, pl.ds(0, CT))

            sent.append(n)
            if len(sent) >= 4 and len(sent) % 2 == 0:
                t_step(1, sent[passed])
                passed += 1
            if len(sent) >= 7 and len(sent) % 3 == 1:
                pump()

    NT = min(C, 512)

    def matmul(b):
        for cg in range(CG):
            rows = pl.ds(pl.multiple_of(b * C + cg * CW, CW), CW)

            def tile(i, c, cg=cg):
                cols = pl.ds(pl.multiple_of(i * NT, NT), NT)
                lhs = tok[b, cg * TC : (cg + 1) * TC].reshape(T, CW)
                part = jnp.dot(lhs, wbuf[rows, cols], preferred_element_type=jnp.float32)
                acc[:, cols] += part
                return c

            lax.fori_loop(0, C // NT, tile, 0)

    def piece(b, cg, h):
        rows = pl.ds(pl.multiple_of(b * C + cg * CW, CW), CW)
        here = slice(h * (T // 2), (h + 1) * (T // 2))

        def tile(i, c):
            cols = pl.ds(pl.multiple_of(i * NT, NT), NT)
            first = cg * TC + h * (TC // 2)
            lhs = tok[b, first : first + TC // 2].reshape(T // 2, CW)
            part = jnp.dot(lhs, wbuf[rows, cols], preferred_element_type=jnp.float32)
            if cg == CG - 1:
                out[here, cols] = (acc[here, cols] + part).astype(jnp.bfloat16)
            else:
                acc[here, cols] += part
            return c

        lax.fori_loop(0, C // NT, tile, 0)

    def multiply(d, here):
        for b in [z] if d == 0 else [z - d, z + d]:
            mine = b // 2 == x

            @pl.when((b >= 0) & (b <= Z - 1) & (mine if here else jnp.logical_not(mine)))
            def _():
                matmul(b)

    for n in sent[passed:]:
        t_step(1, n)
    own_w.wait()
    own_copy(mate_rows).wait_recv()
    multiply(0, True)
    if Z > 2:
        multiply(1, True)
        pump()
        for place, n in enumerate(sent):
            if place in (NB // 2, NB - 3):
                pump()
            t_step(2, n)
    while w_queue:
        pump()
    for fn, e, j in y_queue:
        fn(e, j)

    for d in range(3, Z - 1):
        each(NB, functools.partial(t_step, d))

    for d in range(2, Z - 1):
        multiply(d, True)


    def c_wait(e, j):
        for sign in (-1, 1):
            xb = x + sign * e

            @pl.when((xb >= 0) & (xb <= X - 1))
            def _():
                for h in range(2):
                    c_copy(xb, 1 - core, h, j).wait_recv()

    for e in range(1, X):
        each(WCH, functools.partial(c_wait, e))

    for d in range(Z - 1):
        multiply(d, False)
    if Z == 2:
        multiply(1, True)
        multiply(1, False)
    d = Z - 1

    @pl.when((z > 0) & (z < Z - 1) | (d == 1))
    def _():
        out[...] = acc[...].astype(jnp.bfloat16)

    if d > 1:
        for part in range(2 * CG):
            cg, h = part // 2, 1 - part % 2
            for n in range(cg * TC + h * (TC // 2), cg * TC + (h + 1) * (TC // 2)):
                if d > 2:
                    t_step(d, n)

            @pl.when(z - d >= 0)
            def _():
                piece(z - d, cg, h)

            @pl.when(z + d <= Z - 1)
            def _():
                piece(z + d, cg, h)

    def sent_own_w(j):
        @pl.when(x < X - 1)
        def _():
            x_copy(x, j, 1, True).wait_send()

        @pl.when(x > 0)
        def _():
            x_copy(x, j, -1, True).wait_send()

    @pl.when(r < 2 * X - 1)
    def _():
        h_copy().wait_send()

    each(WCH, sent_own_w)
    own_copy(own_rows).wait_send()

    def w_sent(e, j):
        def left(xb, step, more):
            @pl.when(more)
            def _():
                x_copy(xb, j, step).wait_send()

            y_copy(xb, y, j).wait_send()
            c_copy(xb, core, y, j).wait_send()
            c_copy(xb, core, 1 - y, j).wait_send()

        @pl.when(x - e >= 0)
        def _():
            left(x - e, 1, x < X - 1)

        @pl.when(x + e <= X - 1)
        def _():
            left(x + e, -1, x > 0)

    for e in range(1, X):
        each(WCH, functools.partial(w_sent, e))

    def t_sent(d, n):
        @pl.when((z - d >= 0) & (z < Z - 1))
        def _():
            t_copy(z - d, n, 1).wait_send()

        @pl.when((z + d <= Z - 1) & (z > 0))
        def _():
            t_copy(z + d, n, -1).wait_send()

    for d in range(Z):
        each(NB, functools.partial(t_sent, d))


def local(Z, X, query, keys, values, taps, weight, doc_lengths):
    T, C = query.shape
    R = weight.shape[0]
    n_taps = taps.shape[0]

    CW = min(C, 1024)
    CG, TC = C // CW, T // CT
    NB = CG * TC
    dims = (Z, X, T, C, CW, CG, TC, R, n_taps)
    any_spec = pl.BlockSpec(memory_space=pl.ANY)
    vmem = pl.BlockSpec(memory_space=pltpu.VMEM)
    dma = pltpu.SemaphoreType.DMA
    return pl.pallas_call(
        functools.partial(kernel, dims),
        out_shape=pltpu.VMEM((T, C), jnp.bfloat16),
        in_specs=[any_spec] * 5 + [pl.BlockSpec(memory_space=pltpu.SMEM)],
        out_specs=vmem,
        scratch_shapes=[
            pltpu.VMEM((T, 128), jnp.int32),
            pltpu.VMEM((Z, NB, CT, CW), jnp.bfloat16),
            pltpu.VMEM((2 * X * R, C), jnp.bfloat16),
            pltpu.VMEM((T, C), jnp.float32),
            pltpu.VMEM(((n_taps + T) * 8, 128), jnp.float32),
            pltpu.VMEM(((n_taps + BT) * 8, 128), jnp.float32),
            pltpu.VMEM((BT * 8, 128), jnp.float32),
            pltpu.VMEM((CG, T, CW), jnp.bfloat16),
            pltpu.VMEM((T, CW), jnp.bfloat16),
            pltpu.VMEM((T, CW), jnp.bfloat16),
            pltpu.VMEM((n_taps, CW), jnp.float32),
            pltpu.VMEM((n_taps, C), jnp.bfloat16),
            pltpu.VMEM((n_taps, C), jnp.bfloat16),
            pltpu.VMEM((n_taps, C), jnp.bfloat16),
            pltpu.VMEM((n_taps, C), jnp.bfloat16),
            dma((2, 4, CG)),
            dma((2,)),
            dma((2,)),
            dma((2, Z, NB)),
            dma((Z, NB)),
            dma((2, X, WCH)),
            dma((X, WCH)),
            dma((X, WCH)),
            dma((X, WCH)),
            dma((X, 2, WCH)),
            dma((X, 2, WCH)),
            dma((3,)),
        ],
        compiler_params=pltpu.CompilerParams(
            collective_id=0, has_side_effects=True, vmem_limit_bytes=60 * 2**20
        ),
    )(query, keys, values, weight, taps, doc_lengths)


def solution(mesh):
    placed = (
        P(("groups", "rows"), "cols"),
        P(("groups", "rows"), "cols"),
        P(("groups", "rows"), "cols"),
        P(None, "cols"),
        P("rows", "cols"),
        P("groups"),
    )
    run = functools.partial(local, mesh.shape["cols"], mesh.shape["rows"] // 2)
    return jax.shard_map(
        run, mesh=mesh, in_specs=placed, out_specs=P(("groups", "rows"), "cols"), check_vma=False
    )
```

```python
import functools

import jax
import jax.numpy as jnp
from jax import lax
from jax.experimental import pallas as pl
from jax.experimental.pallas import tpu as pltpu
from jax.sharding import PartitionSpec as P

MESH = pl.DeviceIdType.MESH
BT = 16
CT = 64
WCH = 8


def conv_block(b, starts, xs, hs, ys, n_taps):
    head = jnp.broadcast_to(starts[pl.ds(b, 1), :], (8, 128)) - b

    def history(i, acc):
        k = n_taps // BT - i
        lo = head + k * BT
        base = n_taps + b - k * BT
        taps = [
            hs[pl.ds(pl.multiple_of((k * BT + d) * 8, 8), 8), :] for d in range(1 - BT, BT)
        ]
        acc = list(acc)
        for s in range(BT):
            x = xs[pl.ds(pl.multiple_of((base + s) * 8, 8), 8), :]
            x = jnp.where(lo <= s, x, 0.0)
            for t in range(BT):
                acc[t] = acc[t] + taps[t - s + BT - 1] * x
        return tuple(acc)

    zero = jnp.zeros((8, 128), jnp.float32)
    acc = lax.fori_loop(0, n_taps // BT, history, (zero,) * BT)
    xb = [xs[pl.ds(pl.multiple_of((n_taps + b + s) * 8, 8), 8), :] for s in range(BT)]
    for t in range(BT):
        lo = jnp.broadcast_to(starts[pl.ds(b + t, 1), :], (8, 128)) - b
        total = jnp.where(lo < 0, acc[t], 0.0)
        for s in range(t + 1):
            term = hs[(t - s) * 8 : (t - s) * 8 + 8, :] * xb[s]
            total = total + (term if s == t else jnp.where(lo <= s, term, 0.0))
        ys[t * 8 : t * 8 + 8, :] = total


def kernel(dims, q_hbm, k_hbm, v_hbm, w_hbm, taps_hbm, doc_ref, out, starts, tok, wbuf, acc, xs, hs, ys,
           qs, ks, vs, ts, ktail, vtail, hsend, halo, in_sem, tail_sem, hsem, tsend, trecv, wsend, wrecv, ysend, yrecv, csend, crecv, osem):
    Z, X, T, C, CW, CG, TC, R, n_taps = dims
    NB = CG * TC
    z = lax.axis_index("cols")
    r = lax.axis_index("rows")
    y = lax.axis_index("groups")
    x, core = r // 2, r % 2
    mate = r + 1 - 2 * core
    half, RC = R // 2, R // 2 // WCH

    EARLY = n_taps + CT

    def load(cg):
        cols = pl.ds(cg * CW, CW)
        copies = []
        for part, rows in enumerate((pl.ds(0, EARLY), pl.ds(EARLY, T - EARLY))):
            for i, (src, dst) in enumerate(((k_hbm, ks), (v_hbm, vs), (q_hbm, qs.at[cg]))):
                copies.append((src.at[rows, cols], dst.at[rows], in_sem.at[part, i, cg]))
            if part == 0:
                copies.append((taps_hbm.at[:, cols], ts, in_sem.at[0, 3, cg]))
        return copies

    def begin(copies):
        for src, dst, sem in copies:
            pltpu.make_async_copy(src, dst, sem).start()

    def finish(copies):
        for src, dst, sem in copies:
            pltpu.make_async_copy(src, dst, sem).wait()

    last_rows = pl.ds(T - n_taps, n_taps)
    tails = [
        pltpu.make_async_copy(k_hbm.at[last_rows], ktail, tail_sem.at[0]),
        pltpu.make_async_copy(v_hbm.at[last_rows], vtail, tail_sem.at[1]),
    ]

    begin(load(0)[:4])

    barrier = pltpu.get_barrier_semaphore()

    def greet(cond, who):
        @pl.when(cond)
        def _():
            pl.semaphore_signal(barrier, inc=1, device_id=who, device_id_type=MESH)

    greet(z > 0, {"cols": z - 1})
    greet(z < Z - 1, {"cols": z + 1})
    greet(x > 0, {"rows": r - 2})
    greet(x < X - 1, {"rows": r + 2})
    greet((core == 0) & (x > 0), {"rows": r - 1})
    greet((core == 1) & (x < X - 1), {"rows": r + 1})
    pl.semaphore_signal(barrier, inc=1, device_id={"rows": mate}, device_id_type=MESH)
    pl.semaphore_signal(barrier, inc=1, device_id={"groups": 1 - y}, device_id_type=MESH)
    begin(load(0)[4:])
    for copy in tails:
        copy.start()

    ends = []
    for i in range(doc_ref.shape[0]):
        ends.append(doc_ref[i] + (ends[-1] if ends else 0))

    def mark(i, c):
        rows = pl.ds(pl.multiple_of(i * CT, CT), CT)
        place = lax.broadcasted_iota(jnp.int32, (CT, 128), 0) + (r * T + i * CT)
        start = jnp.zeros((CT, 128), jnp.int32)
        for end in ends:
            start = jnp.where(place >= end, end, start)
        starts[rows, :] = start - r * T
        return c

    lax.fori_loop(0, T // CT, mark, 0)

    spots = jnp.where(z == 0, 1, 0) + jnp.where(z == Z - 1, 1, 0)
    spots = spots + jnp.where(x == 0, 1, 0) + jnp.where(x == X - 1, 1, 0)
    spots = spots + jnp.where((x == 0) & (core == 0), 1, 0)
    spots = spots + jnp.where((x == X - 1) & (core == 1), 1, 0)
    pl.semaphore_wait(barrier, 7 - spots)

    def remote(src, dst, send, recv, who):
        return pltpu.make_async_remote_copy(
            src_ref=src, dst_ref=dst, send_sem=send, recv_sem=recv, device_id=who, device_id_type=MESH
        )

    def h_copy():
        return remote(hsend, halo, hsem.at[0], hsem.at[1], {"rows": r + 1})

    def wrows(rb, h, j):
        return pl.ds(pl.multiple_of(rb * R + h * half + j * RC, 16), RC)

    def x_copy(xb, j, step, own=False):
        rows = wrows(2 * xb + core, y, j)
        src = w_hbm.at[pl.ds(pl.multiple_of(y * half + j * RC, 16), RC)] if own else wbuf.at[rows]
        lane = 0 if step > 0 else 1
        return remote(src, wbuf.at[rows], wsend.at[lane, xb, j], wrecv.at[xb, j], {"rows": r + 2 * step})

    def y_copy(xb, h, j):
        rows = wrows(2 * xb + core, h, j)
        return remote(wbuf.at[rows], wbuf.at[rows], ysend.at[xb, j], yrecv.at[xb, j], {"groups": 1 - y})

    def c_copy(xb, owner, h, j):
        rows = wrows(2 * xb + owner, h, j)
        return remote(wbuf.at[rows], wbuf.at[rows], csend.at[xb, h, j], crecv.at[xb, h, j], {"rows": mate})

    own_rows, mate_rows = pl.ds(r * R, R), pl.ds(mate * R, R)

    def own_copy(rows):
        return remote(w_hbm, wbuf.at[rows], osem.at[1], osem.at[2], {"rows": mate})

    def each(n, fn):
        lax.fori_loop(0, n, lambda i, c: (fn(i), c)[1], 0)

    def send_own_w(j):
        @pl.when(x < X - 1)
        def _():
            x_copy(x, j, 1, True).start()

        @pl.when(x > 0)
        def _():
            x_copy(x, j, -1, True).start()

    own_w = pltpu.make_async_copy(w_hbm, wbuf.at[pl.ds(r * R, R)], osem.at[0])

    def send_others():
        for copy in tails:
            copy.wait()
        tail = ktail[...].astype(jnp.float32) * vtail[...].astype(jnp.float32)
        hsend[...] = tail.astype(jnp.bfloat16)

        @pl.when(r < 2 * X - 1)
        def _():
            h_copy().start()

        each(WCH, send_own_w)
        own_copy(own_rows).start()
        own_w.start()

        @pl.when(r == 0)
        def _():
            halo[...] = jnp.zeros_like(halo)

    def w_step(e, j):
        def pass_on(xb, step, more):
            x_copy(xb, j, step).wait_recv()

            @pl.when(more)
            def _():
                x_copy(xb, j, step).start()

            y_copy(xb, y, j).start()
            c_copy(xb, core, y, j).start()

        @pl.when(x - e >= 0)
        def _():
            pass_on(x - e, 1, x < X - 1)

        @pl.when(x + e <= X - 1)
        def _():
            pass_on(x + e, -1, x > 0)

    def y_step(e, j):
        def pass_on(xb):
            y_copy(xb, 1 - y, j).wait_recv()
            c_copy(xb, core, 1 - y, j).start()

        @pl.when(x - e >= 0)
        def _():
            pass_on(x - e)

        @pl.when(x + e <= X - 1)
        def _():
            pass_on(x + e)

    def t_copy(b, n, step, rows=None):
        part = tok.at[b, n] if rows is None else tok.at[b, n, rows]
        lane = 0 if step > 0 else 1
        return remote(part, part, tsend.at[lane, b, n], trecv.at[b, n], {"cols": z + step})

    def send_own(n, rows):
        @pl.when(z < Z - 1)
        def _():
            t_copy(z, n, 1, rows).start()

        @pl.when(z > 0)
        def _():
            t_copy(z, n, -1, rows).start()

    def t_step(d, n):
        @pl.when(z - d >= 0)
        def _():
            t_copy(z - d, n, 1).wait_recv()

            @pl.when(z < Z - 1)
            def _():
                t_copy(z - d, n, 1).start()

        @pl.when(z + d <= Z - 1)
        def _():
            t_copy(z + d, n, -1).wait_recv()

            @pl.when(z > 0)
            def _():
                t_copy(z + d, n, -1).start()

    w_queue = [(w_step, e, j) for e in range(1, X) for j in range(WCH)]
    y_queue = [(y_step, e, j) for e in range(1, X) for j in range(WCH)]

    def pump():
        if w_queue:
            fn, e, j = w_queue.pop(0)
            fn(e, j)
            if len(y_queue) > len(w_queue) + 1:
                fn, e, j = y_queue.pop(0)
                fn(e, j)

    G = CW // 128
    hs[n_taps * 8 :, :] = jnp.zeros((BT * 8, 128), jnp.float32)
    sent, passed = [], 0
    back = n_taps // CT
    for cg in range(CG):
        finish(load(cg)[: 4 if cg == 0 else None])
        for g in range(G):
            hs[pl.ds(g, n_taps, stride=8), :] = ts[:, g * 128 : g * 128 + 128]

        def fill(tc):
            for g in range(G):
                cols = slice(g * 128, g * 128 + 128)
                rows = pl.ds(pl.multiple_of(tc * CT, CT), CT)
                prod = ks[rows, cols].astype(jnp.float32) * vs[rows, cols].astype(jnp.float32)
                prod = prod.astype(jnp.bfloat16).astype(jnp.float32)
                xs[pl.ds((n_taps + tc * CT) * 8 + g, CT, stride=8), :] = prod

        def chunk(tc, early, cg=cg):
            def block(i, c):
                b = tc * CT + i * BT
                conv_block(b, starts, xs, hs, ys, n_taps)
                rows = pl.ds(pl.multiple_of(b, BT), BT)
                here = pl.ds(pl.multiple_of(i * BT, BT), BT)
                for g in range(G):
                    cols = slice(g * 128, g * 128 + 128)
                    filtered = ys[pl.ds(g, BT, stride=8), :]
                    gate = qs[cg, rows, cols].astype(jnp.float32)
                    tok[z, cg * TC + tc, here, cols] = (gate * filtered).astype(jnp.bfloat16)
                if early:
                    send_own(cg * TC + tc, here)
                return c

            lax.fori_loop(0, CT // BT, block, 0)

        each(back, fill)
        order = list(range(back, TC)) + list(range(back))
        for place, tc in enumerate(order):
            n = cg * TC + tc
            if tc >= back:
                fill(tc)
            if place == TC - back:
                if cg == 0:
                    @pl.when(r > 0)
                    def _():
                        h_copy().wait_recv()

                for g in range(G):
                    c0 = cg * CW + g * 128
                    xs[pl.ds(g, n_taps, stride=8), :] = halo[:, c0 : c0 + 128].astype(jnp.float32)
            if place == TC - back and cg + 1 < CG:
                begin(load(cg + 1))
            early = cg == 0 and place < 6
            chunk(tc, early)
            if not early:
                send_own(n, pl.ds(0, CT))
            if cg == 0 and place == 0:
                send_others()
                finish(load(0)[4:])

            sent.append(n)
            if len(sent) >= 4 and len(sent) % 2 == 0:
                t_step(1, sent[passed])
                passed += 1
            if len(sent) >= 7 and len(sent) % 3 == 1:
                pump()

    NT = min(C, 512)

    def matmul(b):
        for cg in range(CG):
            rows = pl.ds(pl.multiple_of(b * C + cg * CW, CW), CW)

            def tile(i, c, cg=cg):
                cols = pl.ds(pl.multiple_of(i * NT, NT), NT)
                lhs = tok[b, cg * TC : (cg + 1) * TC].reshape(T, CW)
                part = jnp.dot(lhs, wbuf[rows, cols], preferred_element_type=jnp.float32)
                acc[:, cols] += part
                return c

            lax.fori_loop(0, C // NT, tile, 0)

    def piece(b, cg, lo, hi, last):
        rows = pl.ds(pl.multiple_of(b * C + cg * CW, CW), CW)
        here = slice(lo * CT, hi * CT)

        def tile(i, c):
            cols = pl.ds(pl.multiple_of(i * NT, NT), NT)
            lhs = tok[b, cg * TC + lo : cg * TC + hi].reshape((hi - lo) * CT, CW)
            part = jnp.dot(lhs, wbuf[rows, cols], preferred_element_type=jnp.float32)
            if last:
                out[here, cols] = (acc[here, cols] + part).astype(jnp.bfloat16)
            else:
                acc[here, cols] += part
            return c

        lax.fori_loop(0, C // NT, tile, 0)

    def multiply(d, here):
        for b in [z] if d == 0 else [z - d, z + d]:
            mine = b // 2 == x

            @pl.when((b >= 0) & (b <= Z - 1) & (mine if here else jnp.logical_not(mine)))
            def _():
                matmul(b)

    for n in sent[passed:]:
        t_step(1, n)
    acc[...] = jnp.zeros_like(acc)
    own_w.wait()
    own_copy(mate_rows).wait_recv()
    multiply(0, True)
    if Z > 2:
        multiply(1, True)
        pump()
        for place, n in enumerate(sent):
            if place in (NB // 2, NB - 3):
                pump()
            t_step(2, n)
    while w_queue:
        pump()
    for fn, e, j in y_queue:
        fn(e, j)

    for d in range(3, Z - 1):
        each(NB, functools.partial(t_step, d))

    for d in range(2, Z - 1):
        multiply(d, True)


    def c_wait(e, j):
        for sign in (-1, 1):
            xb = x + sign * e

            @pl.when((xb >= 0) & (xb <= X - 1))
            def _():
                for h in range(2):
                    c_copy(xb, 1 - core, h, j).wait_recv()

    for e in range(1, X):
        each(WCH, functools.partial(c_wait, e))

    for d in range(Z - 1):
        multiply(d, False)
    if Z == 2:
        multiply(1, True)
        multiply(1, False)
    d = Z - 1

    @pl.when((z > 0) & (z < Z - 1) | (d == 1))
    def _():
        out[...] = acc[...].astype(jnp.bfloat16)

    if d > 1:
        cuts = [(cg, h * (TC // 2), (h + 1) * (TC // 2)) for cg in range(CG) for h in (1, 0)]
        cuts[-1:] = [(CG - 1, back, TC // 2), (CG - 1, 0, back)]
        for cg, lo, hi in cuts:
            for n in range(cg * TC + lo, cg * TC + hi):
                if d > 2:
                    t_step(d, n)

            @pl.when(z - d >= 0)
            def _():
                piece(z - d, cg, lo, hi, cg == CG - 1)

            @pl.when(z + d <= Z - 1)
            def _():
                piece(z + d, cg, lo, hi, cg == CG - 1)

    def sent_own_w(j):
        @pl.when(x < X - 1)
        def _():
            x_copy(x, j, 1, True).wait_send()

        @pl.when(x > 0)
        def _():
            x_copy(x, j, -1, True).wait_send()

    @pl.when(r < 2 * X - 1)
    def _():
        h_copy().wait_send()

    each(WCH, sent_own_w)
    own_copy(own_rows).wait_send()

    def w_sent(e, j):
        def left(xb, step, more):
            @pl.when(more)
            def _():
                x_copy(xb, j, step).wait_send()

            y_copy(xb, y, j).wait_send()
            c_copy(xb, core, y, j).wait_send()
            c_copy(xb, core, 1 - y, j).wait_send()

        @pl.when(x - e >= 0)
        def _():
            left(x - e, 1, x < X - 1)

        @pl.when(x + e <= X - 1)
        def _():
            left(x + e, -1, x > 0)

    for e in range(1, X):
        each(WCH, functools.partial(w_sent, e))

    def t_sent(d, n):
        @pl.when((z - d >= 0) & (z < Z - 1))
        def _():
            t_copy(z - d, n, 1).wait_send()

        @pl.when((z + d <= Z - 1) & (z > 0))
        def _():
            t_copy(z + d, n, -1).wait_send()

    for d in range(Z):
        each(NB, functools.partial(t_sent, d))


def local(Z, X, query, keys, values, taps, weight, doc_lengths):
    T, C = query.shape
    R = weight.shape[0]
    n_taps = taps.shape[0]

    CW = min(C, 1024)
    CG, TC = C // CW, T // CT
    NB = CG * TC
    dims = (Z, X, T, C, CW, CG, TC, R, n_taps)
    any_spec = pl.BlockSpec(memory_space=pl.ANY)
    vmem = pl.BlockSpec(memory_space=pltpu.VMEM)
    dma = pltpu.SemaphoreType.DMA
    return pl.pallas_call(
        functools.partial(kernel, dims),
        out_shape=pltpu.VMEM((T, C), jnp.bfloat16),
        in_specs=[any_spec] * 5 + [pl.BlockSpec(memory_space=pltpu.SMEM)],
        out_specs=vmem,
        scratch_shapes=[
            pltpu.VMEM((T, 128), jnp.int32),
            pltpu.VMEM((Z, NB, CT, CW), jnp.bfloat16),
            pltpu.VMEM((2 * X * R, C), jnp.bfloat16),
            pltpu.VMEM((T, C), jnp.float32),
            pltpu.VMEM(((n_taps + T) * 8, 128), jnp.float32),
            pltpu.VMEM(((n_taps + BT) * 8, 128), jnp.float32),
            pltpu.VMEM((BT * 8, 128), jnp.float32),
            pltpu.VMEM((CG, T, CW), jnp.bfloat16),
            pltpu.VMEM((T, CW), jnp.bfloat16),
            pltpu.VMEM((T, CW), jnp.bfloat16),
            pltpu.VMEM((n_taps, CW), jnp.float32),
            pltpu.VMEM((n_taps, C), jnp.bfloat16),
            pltpu.VMEM((n_taps, C), jnp.bfloat16),
            pltpu.VMEM((n_taps, C), jnp.bfloat16),
            pltpu.VMEM((n_taps, C), jnp.bfloat16),
            dma((2, 4, CG)),
            dma((2,)),
            dma((2,)),
            dma((2, Z, NB)),
            dma((Z, NB)),
            dma((2, X, WCH)),
            dma((X, WCH)),
            dma((X, WCH)),
            dma((X, WCH)),
            dma((X, 2, WCH)),
            dma((X, 2, WCH)),
            dma((3,)),
        ],
        compiler_params=pltpu.CompilerParams(
            collective_id=0, has_side_effects=True, vmem_limit_bytes=60 * 2**20
        ),
    )(query, keys, values, weight, taps, doc_lengths)


def solution(mesh):
    placed = (
        P(("groups", "rows"), "cols"),
        P(("groups", "rows"), "cols"),
        P(("groups", "rows"), "cols"),
        P(None, "cols"),
        P("rows", "cols"),
        P("groups"),
    )
    run = functools.partial(local, mesh.shape["cols"], mesh.shape["rows"] // 2)
    return jax.shard_map(
        run, mesh=mesh, in_specs=placed, out_specs=P(("groups", "rows"), "cols"), check_vma=False
    )
```

```python
import functools

import jax
import jax.numpy as jnp
from jax import lax
from jax.experimental import pallas as pl
from jax.experimental.pallas import tpu as pltpu
from jax.sharding import PartitionSpec as P

MESH = pl.DeviceIdType.MESH
BT = 16
CT = 64
WCH = 8


def conv_block(b, starts, xs, hs, ys, n_taps):
    head = jnp.broadcast_to(starts[pl.ds(b, 1), :], (8, 128)) - b

    def history(i, acc):
        k = n_taps // BT - i
        lo = head + k * BT
        base = n_taps + b - k * BT
        taps = [
            hs[pl.ds(pl.multiple_of((k * BT + d) * 8, 8), 8), :] for d in range(1 - BT, BT)
        ]
        acc = list(acc)
        for s in range(BT):
            x = xs[pl.ds(pl.multiple_of((base + s) * 8, 8), 8), :]
            x = jnp.where(lo <= s, x, 0.0)
            for t in range(BT):
                acc[t] = acc[t] + taps[t - s + BT - 1] * x
        return tuple(acc)

    zero = jnp.zeros((8, 128), jnp.float32)
    acc = lax.fori_loop(0, n_taps // BT, history, (zero,) * BT)
    xb = [xs[pl.ds(pl.multiple_of((n_taps + b + s) * 8, 8), 8), :] for s in range(BT)]
    for t in range(BT):
        lo = jnp.broadcast_to(starts[pl.ds(b + t, 1), :], (8, 128)) - b
        total = jnp.where(lo < 0, acc[t], 0.0)
        for s in range(t + 1):
            term = hs[(t - s) * 8 : (t - s) * 8 + 8, :] * xb[s]
            total = total + (term if s == t else jnp.where(lo <= s, term, 0.0))
        ys[t * 8 : t * 8 + 8, :] = total


def kernel(dims, q_hbm, k_hbm, v_hbm, w_hbm, taps_hbm, doc_ref, out, starts, tok, wbuf, acc, xs, hs, ys,
           qs, ks, vs, ts, ktail, vtail, hsend, halo, in_sem, tail_sem, hsem, tsend, trecv, wsend, wrecv, ysend, yrecv, csend, crecv, osem):
    Z, X, T, C, CW, CG, TC, R, n_taps = dims
    NB = CG * TC
    z = lax.axis_index("cols")
    r = lax.axis_index("rows")
    y = lax.axis_index("groups")
    x, core = r // 2, r % 2
    mate = r + 1 - 2 * core
    half, RC = R // 2, R // 2 // WCH

    EARLY = n_taps + CT

    def load(cg):
        cols = pl.ds(cg * CW, CW)
        copies = []
        for part, rows in enumerate((pl.ds(0, EARLY), pl.ds(EARLY, T - EARLY))):
            for i, (src, dst) in enumerate(((k_hbm, ks), (v_hbm, vs), (q_hbm, qs.at[cg]))):
                copies.append((src.at[rows, cols], dst.at[rows], in_sem.at[part, i, cg]))
            if part == 0:
                copies.append((taps_hbm.at[:, cols], ts, in_sem.at[0, 3, cg]))
        return copies

    def begin(copies):
        for src, dst, sem in copies:
            pltpu.make_async_copy(src, dst, sem).start()

    def finish(copies):
        for src, dst, sem in copies:
            pltpu.make_async_copy(src, dst, sem).wait()

    last_rows = pl.ds(T - n_taps, n_taps)
    tails = [
        pltpu.make_async_copy(k_hbm.at[last_rows], ktail, tail_sem.at[0]),
        pltpu.make_async_copy(v_hbm.at[last_rows], vtail, tail_sem.at[1]),
    ]

    begin(load(0)[:4])

    barrier = pltpu.get_barrier_semaphore()

    def greet(cond, who):
        @pl.when(cond)
        def _():
            pl.semaphore_signal(barrier, inc=1, device_id=who, device_id_type=MESH)

    greet(z > 0, {"cols": z - 1})
    greet(z < Z - 1, {"cols": z + 1})
    greet(x > 0, {"rows": r - 2})
    greet(x < X - 1, {"rows": r + 2})
    greet((core == 0) & (x > 0), {"rows": r - 1})
    greet((core == 1) & (x < X - 1), {"rows": r + 1})
    pl.semaphore_signal(barrier, inc=1, device_id={"rows": mate}, device_id_type=MESH)
    pl.semaphore_signal(barrier, inc=1, device_id={"groups": 1 - y}, device_id_type=MESH)
    begin(load(0)[4:])
    for copy in tails:
        copy.start()

    ends = []
    for i in range(doc_ref.shape[0]):
        ends.append(doc_ref[i] + (ends[-1] if ends else 0))

    def mark(i, c):
        rows = pl.ds(pl.multiple_of(i * CT, CT), CT)
        place = lax.broadcasted_iota(jnp.int32, (CT, 128), 0) + (r * T + i * CT)
        start = jnp.zeros((CT, 128), jnp.int32)
        for end in ends:
            start = jnp.where(place >= end, end, start)
        starts[rows, :] = start - r * T
        return c

    lax.fori_loop(0, T // CT, mark, 0)

    spots = jnp.where(z == 0, 1, 0) + jnp.where(z == Z - 1, 1, 0)
    spots = spots + jnp.where(x == 0, 1, 0) + jnp.where(x == X - 1, 1, 0)
    spots = spots + jnp.where((x == 0) & (core == 0), 1, 0)
    spots = spots + jnp.where((x == X - 1) & (core == 1), 1, 0)

    def remote(src, dst, send, recv, who):
        return pltpu.make_async_remote_copy(
            src_ref=src, dst_ref=dst, send_sem=send, recv_sem=recv, device_id=who, device_id_type=MESH
        )

    def h_copy():
        return remote(hsend, halo, hsem.at[0], hsem.at[1], {"rows": r + 1})

    def wrows(rb, h, j):
        return pl.ds(pl.multiple_of(rb * R + h * half + j * RC, 16), RC)

    def x_copy(xb, j, step, own=False):
        rows = wrows(2 * xb + core, y, j)
        src = w_hbm.at[pl.ds(pl.multiple_of(y * half + j * RC, 16), RC)] if own else wbuf.at[rows]
        lane = 0 if step > 0 else 1
        return remote(src, wbuf.at[rows], wsend.at[lane, xb, j], wrecv.at[xb, j], {"rows": r + 2 * step})

    def y_copy(xb, h, j):
        rows = wrows(2 * xb + core, h, j)
        return remote(wbuf.at[rows], wbuf.at[rows], ysend.at[xb, j], yrecv.at[xb, j], {"groups": 1 - y})

    def c_copy(xb, owner, h, j):
        rows = wrows(2 * xb + owner, h, j)
        return remote(wbuf.at[rows], wbuf.at[rows], csend.at[xb, h, j], crecv.at[xb, h, j], {"rows": mate})

    own_rows, mate_rows = pl.ds(r * R, R), pl.ds(mate * R, R)

    def own_copy(rows):
        return remote(w_hbm, wbuf.at[rows], osem.at[1], osem.at[2], {"rows": mate})

    def each(n, fn):
        lax.fori_loop(0, n, lambda i, c: (fn(i), c)[1], 0)

    def send_own_w(j):
        @pl.when(x < X - 1)
        def _():
            x_copy(x, j, 1, True).start()

        @pl.when(x > 0)
        def _():
            x_copy(x, j, -1, True).start()

    own_w = pltpu.make_async_copy(w_hbm, wbuf.at[pl.ds(r * R, R)], osem.at[0])

    def send_others():
        for copy in tails:
            copy.wait()
        tail = ktail[...].astype(jnp.float32) * vtail[...].astype(jnp.float32)
        hsend[...] = tail.astype(jnp.bfloat16)

        @pl.when(r < 2 * X - 1)
        def _():
            h_copy().start()

        each(WCH, send_own_w)
        own_copy(own_rows).start()
        own_w.start()

        @pl.when(r == 0)
        def _():
            halo[...] = jnp.zeros_like(halo)

    def w_step(e, j):
        def pass_on(xb, step, more):
            x_copy(xb, j, step).wait_recv()

            @pl.when(more)
            def _():
                x_copy(xb, j, step).start()

            y_copy(xb, y, j).start()
            c_copy(xb, core, y, j).start()

        @pl.when(x - e >= 0)
        def _():
            pass_on(x - e, 1, x < X - 1)

        @pl.when(x + e <= X - 1)
        def _():
            pass_on(x + e, -1, x > 0)

    def y_step(e, j):
        def pass_on(xb):
            y_copy(xb, 1 - y, j).wait_recv()
            c_copy(xb, core, 1 - y, j).start()

        @pl.when(x - e >= 0)
        def _():
            pass_on(x - e)

        @pl.when(x + e <= X - 1)
        def _():
            pass_on(x + e)

    def t_copy(b, n, step, rows=None):
        part = tok.at[b, n] if rows is None else tok.at[b, n, rows]
        lane = 0 if step > 0 else 1
        return remote(part, part, tsend.at[lane, b, n], trecv.at[b, n], {"cols": z + step})

    def send_own(n, rows):
        @pl.when(z < Z - 1)
        def _():
            t_copy(z, n, 1, rows).start()

        @pl.when(z > 0)
        def _():
            t_copy(z, n, -1, rows).start()

    def t_step(d, n):
        @pl.when(z - d >= 0)
        def _():
            t_copy(z - d, n, 1).wait_recv()

            @pl.when(z < Z - 1)
            def _():
                t_copy(z - d, n, 1).start()

        @pl.when(z + d <= Z - 1)
        def _():
            t_copy(z + d, n, -1).wait_recv()

            @pl.when(z > 0)
            def _():
                t_copy(z + d, n, -1).start()

    w_queue = [(w_step, e, j) for e in range(1, X) for j in range(WCH)]
    y_queue = [(y_step, e, j) for e in range(1, X) for j in range(WCH)]

    def pump():
        if w_queue:
            fn, e, j = w_queue.pop(0)
            fn(e, j)
            if len(y_queue) > len(w_queue) + 1:
                fn, e, j = y_queue.pop(0)
                fn(e, j)

    G = CW // 128
    hs[n_taps * 8 :, :] = jnp.zeros((BT * 8, 128), jnp.float32)
    sent, passed = [], 0
    back = n_taps // CT
    for cg in range(CG):
        finish(load(cg)[: 4 if cg == 0 else None])
        for g in range(G):
            hs[pl.ds(g, n_taps, stride=8), :] = ts[:, g * 128 : g * 128 + 128]

        def fill(tc):
            for g in range(G):
                cols = slice(g * 128, g * 128 + 128)
                rows = pl.ds(pl.multiple_of(tc * CT, CT), CT)
                prod = ks[rows, cols].astype(jnp.float32) * vs[rows, cols].astype(jnp.float32)
                prod = prod.astype(jnp.bfloat16).astype(jnp.float32)
                xs[pl.ds((n_taps + tc * CT) * 8 + g, CT, stride=8), :] = prod

        def chunk(tc, early, cg=cg):
            def block(i, c):
                b = tc * CT + i * BT
                conv_block(b, starts, xs, hs, ys, n_taps)
                rows = pl.ds(pl.multiple_of(b, BT), BT)
                here = pl.ds(pl.multiple_of(i * BT, BT), BT)
                for g in range(G):
                    cols = slice(g * 128, g * 128 + 128)
                    filtered = ys[pl.ds(g, BT, stride=8), :]
                    gate = qs[cg, rows, cols].astype(jnp.float32)
                    tok[z, cg * TC + tc, here, cols] = (gate * filtered).astype(jnp.bfloat16)
                if early:
                    send_own(cg * TC + tc, here)
                return c

            lax.fori_loop(0, CT // BT, block, 0)

        each(back, fill)
        order = list(range(back, TC)) + list(range(back))
        for place, tc in enumerate(order):
            n = cg * TC + tc
            if tc >= back:
                fill(tc)
            if place == TC - back:
                if cg == 0:
                    @pl.when(r > 0)
                    def _():
                        h_copy().wait_recv()

                for g in range(G):
                    c0 = cg * CW + g * 128
                    xs[pl.ds(g, n_taps, stride=8), :] = halo[:, c0 : c0 + 128].astype(jnp.float32)
            if place == TC - back and cg + 1 < CG:
                begin(load(cg + 1))
            early = cg == 0 and place < 6
            if cg == 0 and place == 0:
                pl.semaphore_wait(barrier, 7 - spots)
            chunk(tc, early)
            if not early:
                send_own(n, pl.ds(0, CT))
            if cg == 0 and place == 0:
                send_others()
                finish(load(0)[4:])

            sent.append(n)
            if len(sent) >= 4 and len(sent) % 2 == 0:
                t_step(1, sent[passed])
                passed += 1
            if len(sent) >= 7 and len(sent) % 3 == 1:
                pump()

    NT = min(C, 512)

    def matmul(b):
        for cg in range(CG):
            rows = pl.ds(pl.multiple_of(b * C + cg * CW, CW), CW)

            def tile(i, c, cg=cg):
                cols = pl.ds(pl.multiple_of(i * NT, NT), NT)
                lhs = tok[b, cg * TC : (cg + 1) * TC].reshape(T, CW)
                part = jnp.dot(lhs, wbuf[rows, cols], preferred_element_type=jnp.float32)
                acc[:, cols] += part
                return c

            lax.fori_loop(0, C // NT, tile, 0)

    def piece(b, cg, lo, hi, last):
        rows = pl.ds(pl.multiple_of(b * C + cg * CW, CW), CW)
        here = slice(lo * CT, hi * CT)

        def tile(i, c):
            cols = pl.ds(pl.multiple_of(i * NT, NT), NT)
            lhs = tok[b, cg * TC + lo : cg * TC + hi].reshape((hi - lo) * CT, CW)
            part = jnp.dot(lhs, wbuf[rows, cols], preferred_element_type=jnp.float32)
            if last:
                out[here, cols] = (acc[here, cols] + part).astype(jnp.bfloat16)
            else:
                acc[here, cols] += part
            return c

        lax.fori_loop(0, C // NT, tile, 0)

    def multiply(d, here):
        for b in [z] if d == 0 else [z - d, z + d]:
            mine = b // 2 == x

            @pl.when((b >= 0) & (b <= Z - 1) & (mine if here else jnp.logical_not(mine)))
            def _():
                matmul(b)

    for n in sent[passed:]:
        t_step(1, n)
    acc[...] = jnp.zeros_like(acc)
    own_w.wait()
    own_copy(mate_rows).wait_recv()
    multiply(0, True)
    if Z > 2:
        multiply(1, True)
        pump()
        for place, n in enumerate(sent):
            if place in (NB // 2, NB - 3):
                pump()
            t_step(2, n)
    while w_queue:
        pump()
    for fn, e, j in y_queue:
        fn(e, j)

    for d in range(3, Z - 1):
        each(NB, functools.partial(t_step, d))

    for d in range(2, Z - 1):
        multiply(d, True)


    def c_wait(e, j):
        for sign in (-1, 1):
            xb = x + sign * e

            @pl.when((xb >= 0) & (xb <= X - 1))
            def _():
                for h in range(2):
                    c_copy(xb, 1 - core, h, j).wait_recv()

    for e in range(1, X):
        each(WCH, functools.partial(c_wait, e))

    for d in range(Z - 1):
        multiply(d, False)
    if Z == 2:
        multiply(1, True)
        multiply(1, False)
    def all_sent():
        def sent_own_w(j):
            @pl.when(x < X - 1)
            def _():
                x_copy(x, j, 1, True).wait_send()

            @pl.when(x > 0)
            def _():
                x_copy(x, j, -1, True).wait_send()

        @pl.when(r < 2 * X - 1)
        def _():
            h_copy().wait_send()

        each(WCH, sent_own_w)
        own_copy(own_rows).wait_send()

        def w_sent(e, j):
            def left(xb, step, more):
                @pl.when(more)
                def _():
                    x_copy(xb, j, step).wait_send()

                y_copy(xb, y, j).wait_send()
                c_copy(xb, core, y, j).wait_send()
                c_copy(xb, core, 1 - y, j).wait_send()

            @pl.when(x - e >= 0)
            def _():
                left(x - e, 1, x < X - 1)

            @pl.when(x + e <= X - 1)
            def _():
                left(x + e, -1, x > 0)

        for e in range(1, X):
            each(WCH, functools.partial(w_sent, e))

        def t_sent(d, n):
            @pl.when((z - d >= 0) & (z < Z - 1))
            def _():
                t_copy(z - d, n, 1).wait_send()

            @pl.when((z + d <= Z - 1) & (z > 0))
            def _():
                t_copy(z + d, n, -1).wait_send()

        for d in range(Z):
            each(NB, functools.partial(t_sent, d))

    d = Z - 1

    @pl.when((z > 0) & (z < Z - 1) | (d == 1))
    def _():
        out[...] = acc[...].astype(jnp.bfloat16)

    if d > 1:
        cuts = [(cg, h * (TC // 2), (h + 1) * (TC // 2)) for cg in range(CG) for h in (1, 0)]
        cuts[-1:] = [(CG - 1, back, TC // 2), (CG - 1, 0, back)]
        for spot, (cg, lo, hi) in enumerate(cuts):
            if spot == len(cuts) - 3:
                all_sent()
            for n in range(cg * TC + lo, cg * TC + hi):
                if d > 2:
                    t_step(d, n)

            @pl.when(z - d >= 0)
            def _():
                piece(z - d, cg, lo, hi, cg == CG - 1)

            @pl.when(z + d <= Z - 1)
            def _():
                piece(z + d, cg, lo, hi, cg == CG - 1)
    else:
        all_sent()


def local(Z, X, query, keys, values, taps, weight, doc_lengths):
    T, C = query.shape
    R = weight.shape[0]
    n_taps = taps.shape[0]

    CW = min(C, 1024)
    CG, TC = C // CW, T // CT
    NB = CG * TC
    dims = (Z, X, T, C, CW, CG, TC, R, n_taps)
    any_spec = pl.BlockSpec(memory_space=pl.ANY)
    vmem = pl.BlockSpec(memory_space=pltpu.VMEM)
    dma = pltpu.SemaphoreType.DMA
    return pl.pallas_call(
        functools.partial(kernel, dims),
        out_shape=pltpu.VMEM((T, C), jnp.bfloat16),
        in_specs=[any_spec] * 5 + [pl.BlockSpec(memory_space=pltpu.SMEM)],
        out_specs=vmem,
        scratch_shapes=[
            pltpu.VMEM((T, 128), jnp.int32),
            pltpu.VMEM((Z, NB, CT, CW), jnp.bfloat16),
            pltpu.VMEM((2 * X * R, C), jnp.bfloat16),
            pltpu.VMEM((T, C), jnp.float32),
            pltpu.VMEM(((n_taps + T) * 8, 128), jnp.float32),
            pltpu.VMEM(((n_taps + BT) * 8, 128), jnp.float32),
            pltpu.VMEM((BT * 8, 128), jnp.float32),
            pltpu.VMEM((CG, T, CW), jnp.bfloat16),
            pltpu.VMEM((T, CW), jnp.bfloat16),
            pltpu.VMEM((T, CW), jnp.bfloat16),
            pltpu.VMEM((n_taps, CW), jnp.float32),
            pltpu.VMEM((n_taps, C), jnp.bfloat16),
            pltpu.VMEM((n_taps, C), jnp.bfloat16),
            pltpu.VMEM((n_taps, C), jnp.bfloat16),
            pltpu.VMEM((n_taps, C), jnp.bfloat16),
            dma((2, 4, CG)),
            dma((2,)),
            dma((2,)),
            dma((2, Z, NB)),
            dma((Z, NB)),
            dma((2, X, WCH)),
            dma((X, WCH)),
            dma((X, WCH)),
            dma((X, WCH)),
            dma((X, 2, WCH)),
            dma((X, 2, WCH)),
            dma((3,)),
        ],
        compiler_params=pltpu.CompilerParams(
            collective_id=0, has_side_effects=True, vmem_limit_bytes=60 * 2**20
        ),
    )(query, keys, values, weight, taps, doc_lengths)


def solution(mesh):
    placed = (
        P(("groups", "rows"), "cols"),
        P(("groups", "rows"), "cols"),
        P(("groups", "rows"), "cols"),
        P(None, "cols"),
        P("rows", "cols"),
        P("groups"),
    )
    run = functools.partial(local, mesh.shape["cols"], mesh.shape["rows"] // 2)
    return jax.shard_map(
        run, mesh=mesh, in_specs=placed, out_specs=P(("groups", "rows"), "cols"), check_vma=False
    )
```

```python
import functools

import jax
import jax.numpy as jnp
from jax import lax
from jax.experimental import pallas as pl
from jax.experimental.pallas import tpu as pltpu
from jax.sharding import PartitionSpec as P

MESH = pl.DeviceIdType.MESH
BT = 16
CT = 64
WCH = 8


def conv_block(b, starts, xs, hs, ys, n_taps):
    head = jnp.broadcast_to(starts[pl.ds(b, 1), :], (8, 128)) - b

    def history(i, acc):
        k = n_taps // BT - i
        lo = head + k * BT
        base = n_taps + b - k * BT
        taps = [
            hs[pl.ds(pl.multiple_of((k * BT + d) * 8, 8), 8), :] for d in range(1 - BT, BT)
        ]
        acc = list(acc)
        for s in range(BT):
            x = xs[pl.ds(pl.multiple_of((base + s) * 8, 8), 8), :]
            x = jnp.where(lo <= s, x, 0.0)
            for t in range(BT):
                acc[t] = acc[t] + taps[t - s + BT - 1] * x
        return tuple(acc)

    zero = jnp.zeros((8, 128), jnp.float32)
    acc = lax.fori_loop(0, n_taps // BT, history, (zero,) * BT)
    xb = [xs[pl.ds(pl.multiple_of((n_taps + b + s) * 8, 8), 8), :] for s in range(BT)]
    for t in range(BT):
        lo = jnp.broadcast_to(starts[pl.ds(b + t, 1), :], (8, 128)) - b
        total = jnp.where(lo < 0, acc[t], 0.0)
        for s in range(t + 1):
            term = hs[(t - s) * 8 : (t - s) * 8 + 8, :] * xb[s]
            total = total + (term if s == t else jnp.where(lo <= s, term, 0.0))
        ys[t * 8 : t * 8 + 8, :] = total


def kernel(dims, q_hbm, k_hbm, v_hbm, w_hbm, taps_hbm, doc_ref, out, starts, tok, wbuf, acc, xs, hs, ys,
           qs, ks, vs, ts, ktail, vtail, hsend, halo, in_sem, tail_sem, hsem, tsend, trecv, wsend, wrecv, ysend, yrecv, csend, crecv, osem):
    Z, X, T, C, CW, CG, TC, R, n_taps = dims
    NB = CG * TC
    z = lax.axis_index("cols")
    r = lax.axis_index("rows")
    y = lax.axis_index("groups")
    x, core = r // 2, r % 2
    mate = r + 1 - 2 * core
    half, RC = R // 2, R // 2 // WCH

    EARLY = n_taps + CT

    def load(cg):
        cols = pl.ds(cg * CW, CW)
        copies = []
        for part, rows in enumerate((pl.ds(0, EARLY), pl.ds(EARLY, T - EARLY))):
            for i, (src, dst) in enumerate(((k_hbm, ks), (v_hbm, vs), (q_hbm, qs.at[cg]))):
                copies.append((src.at[rows, cols], dst.at[rows], in_sem.at[part, i, cg]))
            if part == 0:
                copies.append((taps_hbm.at[:, cols], ts, in_sem.at[0, 3, cg]))
        return copies

    def begin(copies):
        for src, dst, sem in copies:
            pltpu.make_async_copy(src, dst, sem).start()

    def finish(copies):
        for src, dst, sem in copies:
            pltpu.make_async_copy(src, dst, sem).wait()

    last_rows = pl.ds(T - n_taps, n_taps)
    tails = [
        pltpu.make_async_copy(k_hbm.at[last_rows], ktail, tail_sem.at[0]),
        pltpu.make_async_copy(v_hbm.at[last_rows], vtail, tail_sem.at[1]),
    ]

    begin(load(0)[:4])

    barrier = pltpu.get_barrier_semaphore()

    def greet(cond, who):
        @pl.when(cond)
        def _():
            pl.semaphore_signal(barrier, inc=1, device_id=who, device_id_type=MESH)

    greet(z > 0, {"cols": z - 1})
    greet(z < Z - 1, {"cols": z + 1})
    greet(x > 0, {"rows": r - 2})
    greet(x < X - 1, {"rows": r + 2})
    greet((core == 0) & (x > 0), {"rows": r - 1})
    greet((core == 1) & (x < X - 1), {"rows": r + 1})
    pl.semaphore_signal(barrier, inc=1, device_id={"rows": mate}, device_id_type=MESH)
    pl.semaphore_signal(barrier, inc=1, device_id={"groups": 1 - y}, device_id_type=MESH)
    begin(load(0)[4:])
    for copy in tails:
        copy.start()

    ends = []
    for i in range(doc_ref.shape[0]):
        ends.append(doc_ref[i] + (ends[-1] if ends else 0))

    def mark(i, c):
        rows = pl.ds(pl.multiple_of(i * CT, CT), CT)
        place = lax.broadcasted_iota(jnp.int32, (CT, 128), 0) + (r * T + i * CT)
        start = jnp.zeros((CT, 128), jnp.int32)
        for end in ends:
            start = jnp.where(place >= end, end, start)
        starts[rows, :] = start - r * T
        return c

    lax.fori_loop(0, T // CT, mark, 0)

    spots = jnp.where(z == 0, 1, 0) + jnp.where(z == Z - 1, 1, 0)
    spots = spots + jnp.where(x == 0, 1, 0) + jnp.where(x == X - 1, 1, 0)
    spots = spots + jnp.where((x == 0) & (core == 0), 1, 0)
    spots = spots + jnp.where((x == X - 1) & (core == 1), 1, 0)

    def remote(src, dst, send, recv, who):
        return pltpu.make_async_remote_copy(
            src_ref=src, dst_ref=dst, send_sem=send, recv_sem=recv, device_id=who, device_id_type=MESH
        )

    def h_copy():
        return remote(hsend, halo, hsem.at[0], hsem.at[1], {"rows": r + 1})

    def wrows(rb, h, j):
        return pl.ds(pl.multiple_of(rb * R + h * half + j * RC, 16), RC)

    def x_copy(xb, j, step, own=False):
        rows = wrows(2 * xb + core, y, j)
        src = w_hbm.at[pl.ds(pl.multiple_of(y * half + j * RC, 16), RC)] if own else wbuf.at[rows]
        lane = 0 if step > 0 else 1
        return remote(src, wbuf.at[rows], wsend.at[lane, xb, j], wrecv.at[xb, j], {"rows": r + 2 * step})

    def y_copy(xb, h, j):
        rows = wrows(2 * xb + core, h, j)
        return remote(wbuf.at[rows], wbuf.at[rows], ysend.at[xb, j], yrecv.at[xb, j], {"groups": 1 - y})

    def c_copy(xb, owner, h, j):
        rows = wrows(2 * xb + owner, h, j)
        return remote(wbuf.at[rows], wbuf.at[rows], csend.at[xb, h, j], crecv.at[xb, h, j], {"rows": mate})

    own_rows, mate_rows = pl.ds(r * R, R), pl.ds(mate * R, R)

    def own_copy(rows):
        return remote(w_hbm, wbuf.at[rows], osem.at[1], osem.at[2], {"rows": mate})

    def each(n, fn):
        lax.fori_loop(0, n, lambda i, c: (fn(i), c)[1], 0)

    def send_own_w(j):
        @pl.when(x < X - 1)
        def _():
            x_copy(x, j, 1, True).start()

        @pl.when(x > 0)
        def _():
            x_copy(x, j, -1, True).start()

    own_w = pltpu.make_async_copy(w_hbm, wbuf.at[pl.ds(r * R, R)], osem.at[0])

    def send_others():
        for copy in tails:
            copy.wait()
        tail = ktail[...].astype(jnp.float32) * vtail[...].astype(jnp.float32)
        hsend[...] = tail.astype(jnp.bfloat16)

        @pl.when(r < 2 * X - 1)
        def _():
            h_copy().start()

        each(WCH, send_own_w)
        own_copy(own_rows).start()
        own_w.start()

        @pl.when(r == 0)
        def _():
            halo[...] = jnp.zeros_like(halo)

    def w_step(e, j):
        def pass_on(xb, step, more):
            x_copy(xb, j, step).wait_recv()

            @pl.when(more)
            def _():
                x_copy(xb, j, step).start()

            y_copy(xb, y, j).start()
            c_copy(xb, core, y, j).start()

        @pl.when(x - e >= 0)
        def _():
            pass_on(x - e, 1, x < X - 1)

        @pl.when(x + e <= X - 1)
        def _():
            pass_on(x + e, -1, x > 0)

    def y_step(e, j):
        def pass_on(xb):
            y_copy(xb, 1 - y, j).wait_recv()
            c_copy(xb, core, 1 - y, j).start()

        @pl.when(x - e >= 0)
        def _():
            pass_on(x - e)

        @pl.when(x + e <= X - 1)
        def _():
            pass_on(x + e)

    def t_copy(b, n, step, rows=None):
        part = tok.at[b, n] if rows is None else tok.at[b, n, rows]
        lane = 0 if step > 0 else 1
        return remote(part, part, tsend.at[lane, b, n], trecv.at[b, n], {"cols": z + step})

    def send_own(n, rows):
        @pl.when(z < Z - 1)
        def _():
            t_copy(z, n, 1, rows).start()

        @pl.when(z > 0)
        def _():
            t_copy(z, n, -1, rows).start()

    def t_step(d, n):
        @pl.when(z - d >= 0)
        def _():
            t_copy(z - d, n, 1).wait_recv()

            @pl.when(z < Z - 1)
            def _():
                t_copy(z - d, n, 1).start()

        @pl.when(z + d <= Z - 1)
        def _():
            t_copy(z + d, n, -1).wait_recv()

            @pl.when(z > 0)
            def _():
                t_copy(z + d, n, -1).start()

    w_queue = [(w_step, e, j) for e in range(1, X) for j in range(WCH)]
    y_queue = [(y_step, e, j) for e in range(1, X) for j in range(WCH)]

    def pump():
        if w_queue:
            fn, e, j = w_queue.pop(0)
            fn(e, j)
            if len(y_queue) > len(w_queue) + 1:
                fn, e, j = y_queue.pop(0)
                fn(e, j)

    G = CW // 128
    hs[n_taps * 8 :, :] = jnp.zeros((BT * 8, 128), jnp.float32)
    sent, passed = [], 0
    back = n_taps // CT
    for cg in range(CG):
        finish(load(cg)[: 4 if cg == 0 else None])
        for g in range(G):
            hs[pl.ds(g, n_taps, stride=8), :] = ts[:, g * 128 : g * 128 + 128]

        def fill(tc):
            for g in range(G):
                cols = slice(g * 128, g * 128 + 128)
                rows = pl.ds(pl.multiple_of(tc * CT, CT), CT)
                prod = ks[rows, cols].astype(jnp.float32) * vs[rows, cols].astype(jnp.float32)
                prod = prod.astype(jnp.bfloat16).astype(jnp.float32)
                xs[pl.ds((n_taps + tc * CT) * 8 + g, CT, stride=8), :] = prod

        def chunk(tc, early, cg=cg):
            def block(i, c):
                b = tc * CT + i * BT
                conv_block(b, starts, xs, hs, ys, n_taps)
                rows = pl.ds(pl.multiple_of(b, BT), BT)
                here = pl.ds(pl.multiple_of(i * BT, BT), BT)
                for g in range(G):
                    cols = slice(g * 128, g * 128 + 128)
                    filtered = ys[pl.ds(g, BT, stride=8), :]
                    gate = qs[cg, rows, cols].astype(jnp.float32)
                    tok[z, cg * TC + tc, here, cols] = (gate * filtered).astype(jnp.bfloat16)
                if early:
                    send_own(cg * TC + tc, here)
                return c

            lax.fori_loop(0, CT // BT, block, 0)

        each(back, fill)
        order = list(range(back, TC)) + list(range(back))
        for place, tc in enumerate(order):
            n = cg * TC + tc
            if tc >= back:
                fill(tc)
            if place == TC - back:
                if cg == 0:
                    @pl.when(r > 0)
                    def _():
                        h_copy().wait_recv()

                for g in range(G):
                    c0 = cg * CW + g * 128
                    xs[pl.ds(g, n_taps, stride=8), :] = halo[:, c0 : c0 + 128].astype(jnp.float32)
            if place == TC - back and cg + 1 < CG:
                begin(load(cg + 1))
            early = cg == 0 and place < 6
            if cg == 0 and place == 0:
                pl.semaphore_wait(barrier, 7 - spots)
            chunk(tc, early)
            if not early:
                send_own(n, pl.ds(0, CT))
            if cg == 0 and place == 0:
                finish(load(0)[4:])
            if cg == 0 and place == 1:
                send_others()

            sent.append(n)
            if len(sent) >= 4 and len(sent) % 2 == 0:
                t_step(1, sent[passed])
                passed += 1
            if len(sent) >= 7 and len(sent) % 3 == 1:
                pump()

    NT = min(C, 512)

    def matmul(b):
        for cg in range(CG):
            rows = pl.ds(pl.multiple_of(b * C + cg * CW, CW), CW)

            def tile(i, c, cg=cg):
                cols = pl.ds(pl.multiple_of(i * NT, NT), NT)
                lhs = tok[b, cg * TC : (cg + 1) * TC].reshape(T, CW)
                part = jnp.dot(lhs, wbuf[rows, cols], preferred_element_type=jnp.float32)
                acc[:, cols] += part
                return c

            lax.fori_loop(0, C // NT, tile, 0)

    def piece(b, cg, lo, hi, last):
        rows = pl.ds(pl.multiple_of(b * C + cg * CW, CW), CW)
        here = slice(lo * CT, hi * CT)

        def tile(i, c):
            cols = pl.ds(pl.multiple_of(i * NT, NT), NT)
            lhs = tok[b, cg * TC + lo : cg * TC + hi].reshape((hi - lo) * CT, CW)
            part = jnp.dot(lhs, wbuf[rows, cols], preferred_element_type=jnp.float32)
            if last:
                out[here, cols] = (acc[here, cols] + part).astype(jnp.bfloat16)
            else:
                acc[here, cols] += part
            return c

        lax.fori_loop(0, C // NT, tile, 0)

    def multiply(d, here):
        for b in [z] if d == 0 else [z - d, z + d]:
            mine = b // 2 == x

            @pl.when((b >= 0) & (b <= Z - 1) & (mine if here else jnp.logical_not(mine)))
            def _():
                matmul(b)

    for n in sent[passed:]:
        t_step(1, n)
    acc[...] = jnp.zeros_like(acc)
    own_w.wait()
    own_copy(mate_rows).wait_recv()
    multiply(0, True)
    if Z > 2:
        multiply(1, True)
        pump()
        for place, n in enumerate(sent):
            if place in (NB // 2, NB - 3):
                pump()
            t_step(2, n)
    while w_queue:
        pump()
    for fn, e, j in y_queue:
        fn(e, j)

    for d in range(3, Z - 1):
        each(NB, functools.partial(t_step, d))

    for d in range(2, Z - 1):
        multiply(d, True)


    def c_wait(e, j):
        for sign in (-1, 1):
            xb = x + sign * e

            @pl.when((xb >= 0) & (xb <= X - 1))
            def _():
                for h in range(2):
                    c_copy(xb, 1 - core, h, j).wait_recv()

    for e in range(1, X):
        each(WCH, functools.partial(c_wait, e))

    for d in range(Z - 1):
        multiply(d, False)
    if Z == 2:
        multiply(1, True)
        multiply(1, False)
    def all_sent():
        def sent_own_w(j):
            @pl.when(x < X - 1)
            def _():
                x_copy(x, j, 1, True).wait_send()

            @pl.when(x > 0)
            def _():
                x_copy(x, j, -1, True).wait_send()

        @pl.when(r < 2 * X - 1)
        def _():
            h_copy().wait_send()

        each(WCH, sent_own_w)
        own_copy(own_rows).wait_send()

        def w_sent(e, j):
            def left(xb, step, more):
                @pl.when(more)
                def _():
                    x_copy(xb, j, step).wait_send()

                y_copy(xb, y, j).wait_send()
                c_copy(xb, core, y, j).wait_send()
                c_copy(xb, core, 1 - y, j).wait_send()

            @pl.when(x - e >= 0)
            def _():
                left(x - e, 1, x < X - 1)

            @pl.when(x + e <= X - 1)
            def _():
                left(x + e, -1, x > 0)

        for e in range(1, X):
            each(WCH, functools.partial(w_sent, e))

        def t_sent(d, n):
            @pl.when((z - d >= 0) & (z < Z - 1))
            def _():
                t_copy(z - d, n, 1).wait_send()

            @pl.when((z + d <= Z - 1) & (z > 0))
            def _():
                t_copy(z + d, n, -1).wait_send()

        for d in range(Z):
            each(NB, functools.partial(t_sent, d))

    d = Z - 1

    @pl.when((z > 0) & (z < Z - 1) | (d == 1))
    def _():
        out[...] = acc[...].astype(jnp.bfloat16)

    if d > 1:
        cuts = [(cg, h * (TC // 2), (h + 1) * (TC // 2)) for cg in range(CG) for h in (1, 0)]
        cuts[-1:] = [(CG - 1, back, TC // 2), (CG - 1, 0, back)]
        for spot, (cg, lo, hi) in enumerate(cuts):
            if spot == len(cuts) - 3:
                all_sent()
            for n in range(cg * TC + lo, cg * TC + hi):
                if d > 2:
                    t_step(d, n)

            @pl.when(z - d >= 0)
            def _():
                piece(z - d, cg, lo, hi, cg == CG - 1)

            @pl.when(z + d <= Z - 1)
            def _():
                piece(z + d, cg, lo, hi, cg == CG - 1)
    else:
        all_sent()


def local(Z, X, query, keys, values, taps, weight, doc_lengths):
    T, C = query.shape
    R = weight.shape[0]
    n_taps = taps.shape[0]

    CW = min(C, 1024)
    CG, TC = C // CW, T // CT
    NB = CG * TC
    dims = (Z, X, T, C, CW, CG, TC, R, n_taps)
    any_spec = pl.BlockSpec(memory_space=pl.ANY)
    vmem = pl.BlockSpec(memory_space=pltpu.VMEM)
    dma = pltpu.SemaphoreType.DMA
    return pl.pallas_call(
        functools.partial(kernel, dims),
        out_shape=pltpu.VMEM((T, C), jnp.bfloat16),
        in_specs=[any_spec] * 5 + [pl.BlockSpec(memory_space=pltpu.SMEM)],
        out_specs=vmem,
        scratch_shapes=[
            pltpu.VMEM((T, 128), jnp.int32),
            pltpu.VMEM((Z, NB, CT, CW), jnp.bfloat16),
            pltpu.VMEM((2 * X * R, C), jnp.bfloat16),
            pltpu.VMEM((T, C), jnp.float32),
            pltpu.VMEM(((n_taps + T) * 8, 128), jnp.float32),
            pltpu.VMEM(((n_taps + BT) * 8, 128), jnp.float32),
            pltpu.VMEM((BT * 8, 128), jnp.float32),
            pltpu.VMEM((CG, T, CW), jnp.bfloat16),
            pltpu.VMEM((T, CW), jnp.bfloat16),
            pltpu.VMEM((T, CW), jnp.bfloat16),
            pltpu.VMEM((n_taps, CW), jnp.float32),
            pltpu.VMEM((n_taps, C), jnp.bfloat16),
            pltpu.VMEM((n_taps, C), jnp.bfloat16),
            pltpu.VMEM((n_taps, C), jnp.bfloat16),
            pltpu.VMEM((n_taps, C), jnp.bfloat16),
            dma((2, 4, CG)),
            dma((2,)),
            dma((2,)),
            dma((2, Z, NB)),
            dma((Z, NB)),
            dma((2, X, WCH)),
            dma((X, WCH)),
            dma((X, WCH)),
            dma((X, WCH)),
            dma((X, 2, WCH)),
            dma((X, 2, WCH)),
            dma((3,)),
        ],
        compiler_params=pltpu.CompilerParams(
            collective_id=0, has_side_effects=True, vmem_limit_bytes=60 * 2**20
        ),
    )(query, keys, values, weight, taps, doc_lengths)


def solution(mesh):
    placed = (
        P(("groups", "rows"), "cols"),
        P(("groups", "rows"), "cols"),
        P(("groups", "rows"), "cols"),
        P(None, "cols"),
        P("rows", "cols"),
        P("groups"),
    )
    run = functools.partial(local, mesh.shape["cols"], mesh.shape["rows"] // 2)
    return jax.shard_map(
        run, mesh=mesh, in_specs=placed, out_specs=P(("groups", "rows"), "cols"), check_vma=False
    )
```
